32 devices in a mesh: gx: 8 (over y, x, core), gz: 4 (over z).
Axes of the slice: x: 2, y: 2, z: 4, core: 2. Of those that a mesh axis runs over, the one named last changes fastest.
Arguments:
- velocity_old: float32 [3, 64, 64, 128], P(None, 'gx', 'gz'), may hold values from -6 to 6
- source: float32 [3, 64, 64, 128], P(None, 'gx', 'gz'), may hold values from -6 to 6
- diag_coef: float32 [64, 64, 128], P('gx', 'gz'), may hold values from 0.5 to 2
- face_coef: float32 [3, 64, 64, 128], P(None, 'gx', 'gz'), may hold values from 0.2 to 2
- bc_flags: int32 [2, 64, 64], P(None, 'gx', 'gz'), may hold values from 0 to 1
- coarse_map: int32 [64, 64, 128], P('gx', 'gz'), may hold values from 0 to 15
- coarse_inverse: float32 [512, 64], P('gx'), may hold values from -0.1 to 0.3
Outputs:
- velocity: float32 [3, 64, 64, 128], P(None, 'gx', 'gz')
- pressure: float32 [64, 64, 128], P('gx', 'gz')
The draws below stay inside these ranges and needn't reach their ends.
All inputs are finite; a program needn't handle non-finite values.
Results may differ from the reference program's by a relative error of at most 0.0003.
Values sent between devices are 32-bit elements; how exact they have to be, the bound alone decides.
A program may use at most 64 MiB of HBM per device.

```python
import math
import jax
import jax.numpy as jnp
from jax import lax

CX = 8
CZ = 16
NY = 128
COARSE = 16
NX = 64
NZ = 64
GROUP = 64
N_GX = 8
N_GZ = 4


def draw_coarse_inverse(key, part):
    first, second = jax.random.split(jax.random.fold_in(key, 7))
    spread = jnp.clip(jax.random.normal(first, (N_GX * GROUP, GROUP), jnp.float32), -4.0, 4.0) / jnp.sqrt(jnp.float32(GROUP))
    scales = jax.random.uniform(second, (N_GX * GROUP, 1), jnp.float32, 0.05, 0.2)
    identity = jnp.tile(jnp.eye(GROUP, dtype=jnp.float32), (N_GX, 1))
    return ((identity + 0.5 * spread) * scales).astype(jnp.float32)


def plant(array, rng, least, high):
    dims = array.shape
    index_at = [jax.random.randint(jax.random.fold_in(rng, axis), (), 0, dims[axis]) for axis in range(len(dims))]
    array = array.at[tuple(index_at)].set(least)
    longest = dims.index(max(dims))
    index_at[longest] = (index_at[longest] + 1) % dims[longest]
    return array.at[tuple(index_at)].set(high)


def level_of(key, extent, cuts, smallest, largest):
    def one(dim, parts):
        draws = jax.random.uniform(jax.random.fold_in(jax.random.fold_in(key, 6), dim), (parts,), jnp.float32, smallest / len(cuts), largest / len(cuts))
        return jnp.repeat(jnp.exp(draws), extent[dim] // parts).reshape((-1,) + (1,) * (len(extent) - dim - 1))

    level = one(*cuts[0])
    for cut in cuts[1:]:
        level = level * one(*cut)
    return level


def centred(rng, shape, width, limit, shards=(), kind=jnp.bfloat16):
    result = width * jax.random.normal(rng, shape, jnp.float32)
    if shards:
        result = result * level_of(rng, shape, shards, -0.22, 0.18)
    return jnp.clip(result, -limit, limit).astype(kind)


def setup_inputs(seed: int = 0) -> dict:
    splits = jax.random.split(jax.random.key(seed), 8)
    return {
        "velocity_old": centred(splits[0], (3, NX, NZ, NY), 1.0, 6.0, ((1, 8), (2, 4)), jnp.float32),
        "source": centred(splits[1], (3, NX, NZ, NY), 1.0, 6.0, ((1, 8), (2, 4)), jnp.float32),
        "diag_coef": jnp.clip(jnp.exp(math.log(2.0) - 1.3862944 * jax.random.uniform(splits[2], (NX, NZ, NY), jnp.float32) ** level_of(splits[2], (NX, NZ, NY), ((0, 8), (1, 4)), -0.2, 0.2)), 0.5, 2.0),
        "face_coef": jnp.clip(jnp.exp(math.log(2.0) - 2.3025851 * jax.random.uniform(splits[3], (3, NX, NZ, NY), jnp.float32) ** level_of(splits[3], (3, NX, NZ, NY), ((1, 8), (2, 4)), -0.2, 0.2)), 0.2, 2.0),
        "bc_flags": plant(jax.random.randint(splits[4], (2, NX, NZ), 0, 2), jax.random.fold_in(splits[4], 1), 0, 1).astype(jnp.int32),
        "coarse_map": plant(jax.random.randint(splits[5], (NX, NZ, NY), 0, COARSE), jax.random.fold_in(splits[5], 1), 0, COARSE - 1).astype(jnp.int32),
        "coarse_inverse": draw_coarse_inverse(jax.random.fold_in(splits[7], 71), 0),
    }


jacobi_weight = 2.0 / 3.0


def momentum_apply(field, diag_coef, face_coef):
    coef_x, coef_z, coef_y = face_coef[0], face_coef[1], face_coef[2]
    count_y = coef_y.shape[-1]
    level = lax.broadcasted_iota(jnp.int32, coef_y.shape, 2)
    wall = jnp.where((level == 0) | (level == count_y - 1), coef_y[..., -1:], 0.0)
    flux_x = coef_x * (field - jnp.roll(field, -1, axis=1))
    flux_z = coef_z * (field - jnp.roll(field, -1, axis=2))
    planar = (flux_x - jnp.roll(flux_x, 1, axis=1)) + (flux_z - jnp.roll(flux_z, 1, axis=2))
    grad_y = coef_y[..., :-1] * (field[..., :-1] - field[..., 1:])
    zero = jnp.zeros_like(field[..., :1])
    vertical = jnp.concatenate([grad_y, zero], -1) - jnp.concatenate([zero, grad_y], -1) + wall * field
    return diag_coef * field + planar + vertical


def pressure_apply(field, pdiag):
    zero = jnp.zeros_like(field[..., :1])
    beside = (jnp.roll(field, -1, 0) + jnp.roll(field, 1, 0)) + (jnp.roll(field, -1, 1) + jnp.roll(field, 1, 1))
    beside = beside + (jnp.concatenate([field[..., 1:], zero], -1) + jnp.concatenate([zero, field[..., :-1]], -1))
    return pdiag * field - beside


def inner(left, right):
    return jnp.sum(left * right, axis=(1, 2, 3))


def widen(value):
    return value[:, None, None, None]


def reference(velocity_old, source, diag_coef, face_coef, bc_flags, coarse_map, coarse_inverse):
    def apply(field):
        return momentum_apply(field, diag_coef, face_coef)

    x = velocity_old
    r = source - apply(x)
    r0 = r
    p = r
    v = apply(p)
    rho = inner(r0, r0)
    alpha = rho / inner(r0, v)
    s = r - widen(alpha) * v
    t = apply(s)
    omega = inner(t, s) / inner(t, t)
    x = x + widen(alpha) * p + widen(omega) * s
    r = s - widen(omega) * t
    rho_new = inner(r0, s) - omega * inner(r0, t)
    beta = (rho_new / rho) * (alpha / omega)
    p = r + widen(beta) * (p - widen(omega) * v)
    v = apply(p)
    alpha = rho_new / inner(r0, v)
    s = r - widen(alpha) * v
    t = apply(s)
    omega = inner(t, s) / inner(t, t)
    velocity = x + widen(alpha) * p + widen(omega) * s

    along_x, along_z, along_y = velocity[0], velocity[1], velocity[2]
    zero = jnp.zeros_like(along_y[..., :1])
    div = (along_x - jnp.roll(along_x, 1, 0)) + (along_z - jnp.roll(along_z, 1, 1))
    div = div + (along_y - jnp.concatenate([zero, along_y[..., :-1]], -1))
    level = lax.broadcasted_iota(jnp.int32, div.shape, 2)
    flags = bc_flags.astype(jnp.float32)
    bottom = level == 0
    top = level == NY - 1
    pdiag = 6.0 - bottom.astype(jnp.float32) - top.astype(jnp.float32)
    pdiag = pdiag + jnp.where(bottom, flags[0][..., None], 0.0) + jnp.where(top, flags[1][..., None], 0.0)

    q = jacobi_weight * div / pdiag
    q = q + jacobi_weight * (div - pressure_apply(q, pdiag)) / pdiag
    res = div - pressure_apply(q, pdiag)
    block_x = lax.broadcasted_iota(jnp.int32, div.shape, 0) // CX
    block_z = lax.broadcasted_iota(jnp.int32, div.shape, 1) // CZ
    ids = ((block_x * N_GZ + block_z) * COARSE + coarse_map).astype(jnp.int32)
    coarse = jax.ops.segment_sum(res.reshape(-1), ids.reshape(-1), num_segments=N_GX * N_GZ * COARSE)
    coarse = coarse.reshape(N_GX, GROUP)
    blocks = coarse_inverse.reshape(N_GX, GROUP, GROUP)
    corr = jnp.einsum("gab,gb->ga", blocks, coarse, precision=lax.Precision.HIGHEST).reshape(-1)
    q = q + corr[ids]
    for sweep in range(2):
        q = q + jacobi_weight * (div - pressure_apply(q, pdiag)) / pdiag
    return velocity, q
```

```python
import functools

import jax
import jax.numpy as jnp
from jax import lax
from jax.experimental import pallas as pl
from jax.experimental.pallas import tpu as pltpu
from jax.sharding import PartitionSpec as P

COARSE = 16
PAD = 8

jacobi_weight = 2.0 / 3.0
MESH = pl.DeviceIdType.MESH


def kernel(
    dims,
    x0_ref, src_ref, diag_ref, face_ref, bc_ref, map_ref, inv_ref,
    vel_ref, out_ref,
    fld, xlo, xhi, zlo, zhi, zsend,
    coef_send, coef_x, coef_z,
    prs, pxlo, pxhi, pzlo, pzhi, pzsend,
    dgn, cxl, czl, cyu, cyl,
    msg_x, got_x, msg_z, got_z, msg_c, got_c,
    send_sem, recv_sem, coef_ssem, coef_rsem,
    sum_sx, sum_rx, sum_sz, sum_rz, coarse_s, coarse_r,
):
    n_gx, n_gz, cx_n, cz_n, ny, lanes = dims
    rows = cx_n * cz_n
    gx = lax.axis_index("gx")
    gz = lax.axis_index("gz")
    east = (lax.rem(gx + 1, n_gx), gz)
    west = (lax.rem(gx + n_gx - 1, n_gx), gz)
    north = (gx, lax.rem(gz + 1, n_gz))
    south = (gx, lax.rem(gz + n_gz - 1, n_gz))
    row_x = [(lax.rem(gx + d, n_gx), gz) for d in range(1, n_gx)]
    row_z = [(gx, lax.rem(gz + d, n_gz)) for d in range(1, n_gz)]
    pending = []

    def send(src, dst, ssem, rsem, to):
        copy = pltpu.make_async_remote_copy(
            src_ref=src, dst_ref=dst, send_sem=ssem, recv_sem=rsem,
            device_id=to, device_id_type=MESH,
        )
        copy.start()
        pending.append(copy)
        return copy

    barrier = pltpu.get_barrier_semaphore()
    for other in row_x + row_z:
        pl.semaphore_signal(barrier, inc=1, device_id=other, device_id_type=MESH)
    pl.semaphore_wait(barrier, len(row_x) + len(row_z))

    last = rows - cz_n

    def exchange(phase, src, zs, lo_x, hi_x, lo_z, hi_z):
        zs[0] = src[:, pl.ds(cz_n - 1, cx_n, stride=cz_n), :]
        zs[1] = src[:, pl.ds(0, cx_n, stride=cz_n), :]
        sems = [(send_sem.at[phase, i], recv_sem.at[phase, i]) for i in range(4)]
        return [
            send(zs.at[0], lo_z, *sems[2], north),
            send(zs.at[1], hi_z, *sems[3], south),
            send(src.at[:, pl.ds(last, cz_n), :], lo_x, *sems[0], east),
            send(src.at[:, pl.ds(0, cz_n), :], hi_x, *sems[1], west),
        ]

    def exchange_field(i, src):
        return exchange(i, src, zsend.at[i], xlo.at[i], xhi.at[i], zlo.at[i], zhi.at[i])

    def exchange_pressure(i):
        return exchange(
            5 + i, prs.at[i], pzsend.at[i], pxlo.at[i], pxhi.at[i], pzlo.at[i], pzhi.at[i]
        )

    def arrive(copies):
        for copy in copies:
            copy.wait_recv()

    level = lax.broadcasted_iota(jnp.int32, (rows, ny), 1)
    depth = lax.rem(lax.broadcasted_iota(jnp.int32, (rows, ny), 0), cz_n)
    bottom = level == 0
    top = level == ny - 1
    front = depth == 0
    back = depth == cz_n - 1

    def spread(edge):
        wide = jnp.broadcast_to(edge[..., None, :], edge.shape[:-1] + (cz_n, ny))
        return wide.reshape(edge.shape[:-2] + (rows, ny))

    def x_prev(f, edge):
        return jnp.concatenate([edge, f[..., : rows - cz_n, :]], -2)

    def x_next(f, edge):
        return jnp.concatenate([f[..., cz_n:, :], edge], -2)

    def z_prev(f, edge):
        return jnp.where(front, spread(edge), pltpu.roll(f, 1, f.ndim - 2))

    def z_next(f, edge):
        return jnp.where(back, spread(edge), pltpu.roll(f, rows - 1, f.ndim - 2))

    def y_prev(f):
        return pltpu.roll(f, 1, f.ndim - 1)

    def y_next(f):
        return pltpu.roll(f, ny - 1, f.ndim - 1)

    halo0 = exchange_field(0, x0_ref)
    coef_send[...] = face_ref[1, pl.ds(cz_n - 1, cx_n, stride=cz_n), :]
    coefs = [
        send(face_ref.at[0, pl.ds(last, cz_n), :], coef_x, coef_ssem.at[0], coef_rsem.at[0], east),
        send(coef_send, coef_z, coef_ssem.at[1], coef_rsem.at[1], north),
    ]
    cy = face_ref[2]
    upper = jnp.where(top, 0.0, cy)
    lower = jnp.where(bottom, 0.0, y_prev(cy))
    wall = jnp.where(bottom | top, jnp.broadcast_to(cy[:, ny - 1 :], (rows, ny)), 0.0)
    cyu[...] = upper
    cyl[...] = lower
    base = diag_ref[...] + (face_ref[0] + face_ref[1]) + (upper + lower) + wall
    eye = lax.broadcasted_iota(jnp.int32, (cz_n, cz_n), 0) == lax.broadcasted_iota(
        jnp.int32, (cz_n, cz_n), 1
    )

    def column(side):
        flags = bc_ref[side].astype(jnp.float32)
        parts = [
            jnp.sum(
                jnp.where(eye, jnp.broadcast_to(flags[i : i + 1], (cz_n, cz_n)), 0.0),
                axis=1, keepdims=True,
            )
            for i in range(cx_n)
        ]
        return jnp.broadcast_to(jnp.concatenate(parts, 0), (rows, ny))

    arrive(coefs)
    west_c = x_prev(face_ref[0], coef_x[...])
    south_c = z_prev(face_ref[1], coef_z[...])
    cxl[...] = west_c
    czl[...] = south_c
    dgn[...] = base + (west_c + south_c)

    def apply(f, i):
        total = dgn[...] * f
        total -= face_ref[0] * x_next(f, xhi[i]) + cxl[...] * x_prev(f, xlo[i])
        total -= face_ref[1] * z_next(f, zhi[i]) + czl[...] * z_prev(f, zlo[i])
        total -= cyu[...] * y_next(f) + cyl[...] * y_prev(f)
        return total

    def dots(pairs):
        sums = [jnp.sum(a * b, axis=1, keepdims=True) for a, b in pairs]
        while len(sums) < PAD:
            sums.append(jnp.zeros_like(sums[0]))
        stack = jnp.concatenate(sums, 1).reshape(3 * PAD, ny)
        total = jnp.sum(stack, axis=1, keepdims=True)
        shape = (3 * PAD, 128)
        pick = lax.broadcasted_iota(jnp.int32, shape, 0) == lax.broadcasted_iota(
            jnp.int32, shape, 1
        )
        return jnp.sum(
            jnp.where(pick, jnp.broadcast_to(total, shape), 0.0), axis=0, keepdims=True
        )

    def scatter(msg, got, ssem, rsem, others):
        return [
            send(msg, got.at[d], ssem.at[d], rsem, to) for d, to in enumerate(others)
        ]

    def gathered(msg, got, rsem):
        pltpu.make_async_copy(got, got, rsem).wait()
        return msg[...] + jnp.sum(got[...], axis=0)

    def unpack(total):
        shape = (3 * PAD, 128)
        pick = lax.broadcasted_iota(jnp.int32, shape, 0) == lax.broadcasted_iota(
            jnp.int32, shape, 1
        )
        col = jnp.sum(
            jnp.where(pick, jnp.broadcast_to(total, shape), 0.0), axis=1, keepdims=True
        )
        wide = jnp.broadcast_to(col, (3 * PAD, ny)).reshape(3, PAD, ny)
        return [wide[:, k : k + 1] for k in range(PAD)]

    def sums_start(i, pairs):
        msg_x[i] = dots(pairs)
        scatter(msg_x.at[i], got_x.at[i], sum_sx.at[i], sum_rx.at[i], row_x)

    def sums_turn(i):
        msg_z[i] = gathered(msg_x.at[i], got_x.at[i], sum_rx.at[i])
        scatter(msg_z.at[i], got_z.at[i], sum_sz.at[i], sum_rz.at[i], row_z)

    def sums_end(i):
        return unpack(gathered(msg_z.at[i], got_z.at[i], sum_rz.at[i]))

    arrive(halo0)
    fld[1] = src_ref[...] - apply(x0_ref[...], 0)
    halo = exchange_field(1, fld.at[1])
    pdiag = 6.0 - jnp.where(bottom | top, 1.0, 0.0)
    pdiag = pdiag + jnp.where(bottom, column(0), 0.0) + jnp.where(top, column(1), 0.0)
    share = jacobi_weight / pdiag
    arrive(halo)
    fld[2] = apply(fld[1], 1)
    halo = exchange_field(2, fld.at[2])
    arrive(halo)
    fld[3] = apply(fld[2], 2)
    halo = exchange_field(3, fld.at[3])
    r, v, u = fld[1], fld[2], fld[3]
    sums_start(0, [(r, r), (r, v), (r, u), (v, v), (v, u), (u, u)])
    arrive(halo)
    fld[4] = apply(fld[3], 3)
    halo = exchange_field(4, fld.at[4])
    sums_turn(0)
    arrive(halo)
    z = apply(fld[4], 4)
    rr, rv, ru, vv, vu, uu = sums_end(0)[:6]
    alpha = rr / rv
    omega = (rv - alpha * (vv + ru) + alpha * alpha * vu) / (
        vv - 2.0 * alpha * vu + alpha * alpha * uu
    )
    rho_new = (rr - alpha * rv) - omega * (rv - alpha * ru)
    beta = (rho_new / rr) * (alpha / omega)

    def first(x, r, v, u, y, a, w, b):
        s = r - a * v
        t = v - a * u
        x1 = x + a * r + w * s
        r1 = s - w * t
        p2 = r1 + b * (r - w * v)
        mr1 = t - w * (u - a * y)
        v2 = mr1 + b * (v - w * u)
        return x1, r1, p2, v2, mr1

    r, v, u, y = fld[1], fld[2], fld[3], fld[4]
    x1, r1, p2, v2, mr1 = first(x0_ref[...], r, v, u, y, alpha, omega, beta)
    mv2 = (u - alpha * y) - omega * (y - alpha * z) + beta * (u - omega * y)
    sums_start(
        1,
        [(r, v2), (r1, mr1), (r1, mv2), (v2, mr1), (v2, mv2), (mr1, mr1), (mr1, mv2), (mv2, mv2)],
    )
    fld[5] = x1
    fld[6] = r1
    fld[7] = p2
    fld[8] = v2

    def edge_of(buf, c):
        return first(
            *[buf[i, c] for i in range(5)], alpha[c], omega[c], beta[c]
        )[:4]

    edge_x = edge_of(xlo, 0)
    edge_z = edge_of(zlo, 1)
    sums_turn(1)
    rv2, k1, k2, k3, k4, k5, k6, k7 = sums_end(1)
    alpha2 = rho_new / rv2
    omega2 = (k1 - alpha2 * (k2 + k3) + alpha2 * alpha2 * k4) / (
        k5 - 2.0 * alpha2 * k6 + alpha2 * alpha2 * k7
    )

    def second(x1, r1, p2, v2, a, w):
        return x1 + a * p2 + w * (r1 - a * v2)

    velocity = second(fld[5], fld[6], fld[7], fld[8], alpha2, omega2)
    vel_ref[...] = velocity
    west_u = second(*edge_x, alpha2[0], omega2[0])
    south_w = second(*edge_z, alpha2[1], omega2[1])
    ux, uz, uy = velocity[0], velocity[1], velocity[2]
    div = (ux - x_prev(ux, west_u)) + (uz - z_prev(uz, south_w))
    div = div + (uy - jnp.where(bottom, 0.0, y_prev(uy)))

    def beside(f, i):
        near = x_next(f, pxhi[i, 0]) + x_prev(f, pxlo[i, 0])
        near += z_next(f, pzhi[i, 0]) + z_prev(f, pzlo[i, 0])
        return near + (
            jnp.where(top, 0.0, y_next(f)) + jnp.where(bottom, 0.0, y_prev(f))
        )

    def residual(f, i):
        return div - (pdiag * f - beside(f, i))

    q = share * div
    prs[0, 0] = q
    arrive(exchange_pressure(0))
    q = q + share * residual(q, 0)
    prs[1, 0] = q
    arrive(exchange_pressure(1))
    res = residual(q, 1)
    cells = map_ref[...]
    parts = [
        jnp.sum(jnp.where(cells == m, res, 0.0), axis=0, keepdims=True) for m in range(COARSE)
    ]
    total = jnp.sum(jnp.concatenate(parts, 0), axis=1, keepdims=True)
    shape = (COARSE, lanes)
    place = lax.broadcasted_iota(jnp.int32, shape, 1) == (
        lax.broadcasted_iota(jnp.int32, shape, 0) + gz * COARSE
    )
    msg_c[...] = jnp.sum(
        jnp.where(place, jnp.broadcast_to(total, shape), 0.0), axis=0, keepdims=True
    )
    scatter(msg_c, got_c, coarse_s, coarse_r, row_z)
    coarse = gathered(msg_c, got_c, coarse_r)
    own = inv_ref[pl.ds(pl.multiple_of(gz * COARSE, COARSE), COARSE), :]
    corr = jnp.sum(own * coarse[:, : own.shape[1]], axis=1, keepdims=True)
    corr = jnp.broadcast_to(corr, (COARSE, ny))
    add = jnp.broadcast_to(corr[0:1], (rows, ny))
    for m in range(1, COARSE):
        add = jnp.where(cells == m, corr[m : m + 1], add)
    q = q + add
    for i in (2, 3):
        prs[i, 0] = q
        arrive(exchange_pressure(i))
        q = q + share * residual(q, i)
    out_ref[...] = q
    for copy in pending:
        copy.wait_send()


def body(n_gx, n_gz, velocity_old, source, diag_coef, face_coef, bc_flags, coarse_map, coarse_inverse):
    cx_n, cz_n, ny = diag_coef.shape
    rows = cx_n * cz_n
    group = coarse_inverse.shape[1]
    lanes = -(-group // 128) * 128
    f32 = jnp.float32
    vmem = pltpu.VMEM
    dma = pltpu.SemaphoreType.DMA
    scratch = [
        vmem((9, 3, rows, ny), f32),
        vmem((5, 3, cz_n, ny), f32),
        vmem((5, 3, cz_n, ny), f32),
        vmem((5, 3, cx_n, ny), f32),
        vmem((5, 3, cx_n, ny), f32),
        vmem((5, 2, 3, cx_n, ny), f32),
        vmem((cx_n, ny), f32),
        vmem((cz_n, ny), f32),
        vmem((cx_n, ny), f32),
        vmem((4, 1, rows, ny), f32),
        vmem((4, 1, cz_n, ny), f32),
        vmem((4, 1, cz_n, ny), f32),
        vmem((4, 1, cx_n, ny), f32),
        vmem((4, 1, cx_n, ny), f32),
        vmem((4, 2, 1, cx_n, ny), f32),
        vmem((rows, ny), f32),
        vmem((rows, ny), f32),
        vmem((rows, ny), f32),
        vmem((rows, ny), f32),
        vmem((rows, ny), f32),
        vmem((2, 1, 128), f32),
        vmem((2, n_gx - 1, 1, 128), f32),
        vmem((2, 1, 128), f32),
        vmem((2, n_gz - 1, 1, 128), f32),
        vmem((1, lanes), f32),
        vmem((n_gz - 1, 1, lanes), f32),
        dma((9, 4)),
        dma((9, 4)),
        dma((2,)),
        dma((2,)),
        dma((2, n_gx - 1)),
        dma((2,)),
        dma((2, n_gz - 1)),
        dma((2,)),
        dma((n_gz - 1,)),
        dma,
    ]
    spec = pl.BlockSpec(memory_space=pltpu.VMEM)
    velocity, pressure = pl.pallas_call(
        functools.partial(kernel, (n_gx, n_gz, cx_n, cz_n, ny, lanes)),
        out_shape=(
            jax.ShapeDtypeStruct((3, rows, ny), f32),
            jax.ShapeDtypeStruct((rows, ny), f32),
        ),
        in_specs=[spec] * 7,
        out_specs=(spec, spec),
        scratch_shapes=scratch,
        compiler_params=pltpu.CompilerParams(
            collective_id=0, has_side_effects=True, vmem_limit_bytes=48 * 1024 * 1024
        ),
        name="corrector",
    )(
        velocity_old.reshape(3, rows, ny),
        source.reshape(3, rows, ny),
        diag_coef.reshape(rows, ny),
        face_coef.reshape(3, rows, ny),
        bc_flags,
        coarse_map.reshape(rows, ny),
        coarse_inverse,
    )
    return velocity.reshape(3, cx_n, cz_n, ny), pressure.reshape(cx_n, cz_n, ny)


def solution(mesh):
    placed = (
        P(None, "gx", "gz", None),
        P(None, "gx", "gz", None),
        P("gx", "gz", None),
        P(None, "gx", "gz", None),
        P(None, "gx", "gz"),
        P("gx", "gz", None),
        P("gx", None),
    )
    return jax.shard_map(
        functools.partial(body, mesh.shape["gx"], mesh.shape["gz"]),
        mesh=mesh,
        in_specs=placed,
        out_specs=(P(None, "gx", "gz", None), P("gx", "gz", None)),
        check_vma=False,
    )
```

```python
import functools

import jax
import jax.numpy as jnp
from jax import lax
from jax.experimental import pallas as pl
from jax.experimental.pallas import tpu as pltpu
from jax.sharding import PartitionSpec as P

COARSE = 16
PAD = 8

jacobi_weight = 2.0 / 3.0
MESH = pl.DeviceIdType.MESH


def kernel(
    dims,
    x0_in, src_in, diag_in, face_in, bc_in, map_in, inv_in,
    vel_ref, out_ref,
    x0_ref, src_ref, diag_ref, face_ref, bc_ref, map_ref, inv_ref,
    fld, xlo, xhi, zlo, zhi, zsend,
    coef_send, coef_x, coef_z,
    prs, pxlo, pxhi, pzlo, pzhi, pzsend,
    qxlo, qxhi, qzlo, qzhi, qzsend, qc_send, qc,
    mxlo, mxhi, mzlo, mzhi, mzsend, mc_send, mc,
    dxlo, dxhi, dzlo, dzhi, dzsend, inv_w, inv_e,
    dgn, cxl, czl, cyu, cyl,
    msg_x, got_x, msg_z, got_z, msg_c, got_c, got_w, got_e,
    send_sem, recv_sem, coef_ssem, coef_rsem,
    sum_sx, sum_rx, sum_sz, sum_rz, coarse_s, coarse_r,
    load_sem, side_s, side_r,
):
    n_gx, n_gz, cx_n, cz_n, ny, lanes = dims
    rows = cx_n * cz_n
    gx = lax.axis_index("gx")
    gz = lax.axis_index("gz")
    east = (lax.rem(gx + 1, n_gx), gz)
    west = (lax.rem(gx + n_gx - 1, n_gx), gz)
    north = (gx, lax.rem(gz + 1, n_gz))
    south = (gx, lax.rem(gz + n_gz - 1, n_gz))
    row_x = [(lax.rem(gx + d, n_gx), gz) for d in range(1, n_gx)]
    row_z = [(gx, lax.rem(gz + d, n_gz)) for d in range(1, n_gz)]
    pending = []

    def send(src, dst, ssem, rsem, to):
        copy = pltpu.make_async_remote_copy(
            src_ref=src, dst_ref=dst, send_sem=ssem, recv_sem=rsem,
            device_id=to, device_id_type=MESH,
        )
        copy.start()
        pending.append(copy)
        return copy

    aside_w = [(west[0], to[1]) for to in row_z]
    aside_e = [(east[0], to[1]) for to in row_z]
    corners = [
        (east[0], north[1]), (east[0], south[1]), (west[0], north[1]), (west[0], south[1])
    ]
    loads = [
        pltpu.make_async_copy(a, b, load_sem.at[i])
        for i, (a, b) in enumerate(
            [
                (x0_in, x0_ref), (face_in, face_ref), (diag_in, diag_ref), (src_in, src_ref),
                (bc_in, bc_ref), (map_in, map_ref), (inv_in, inv_ref),
            ]
        )
    ]
    for load in loads:
        load.start()
    barrier = pltpu.get_barrier_semaphore()
    partners = row_x + row_z + aside_w + aside_e
    for other in partners:
        pl.semaphore_signal(barrier, inc=1, device_id=other, device_id_type=MESH)
    loads[0].wait()
    loads[1].wait()
    pl.semaphore_wait(barrier, len(partners))

    last = rows - cz_n

    def exchange(phase, src, zs, lo_x, hi_x, lo_z, hi_z):
        zs[0] = src[:, pl.ds(cz_n - 1, cx_n, stride=cz_n), :]
        zs[1] = src[:, pl.ds(0, cx_n, stride=cz_n), :]
        sems = [(send_sem.at[phase, i], recv_sem.at[phase, i]) for i in range(4)]
        return [
            send(zs.at[0], lo_z, *sems[2], north),
            send(zs.at[1], hi_z, *sems[3], south),
            send(src.at[:, pl.ds(last, cz_n), :], lo_x, *sems[0], east),
            send(src.at[:, pl.ds(0, cz_n), :], hi_x, *sems[1], west),
        ]

    def exchange_field(i, src):
        return exchange(i, src, zsend.at[i], xlo.at[i], xhi.at[i], zlo.at[i], zhi.at[i])

    def exchange_pressure(i):
        return exchange(
            5 + i, prs.at[i], pzsend.at[i], pxlo.at[i], pxhi.at[i], pzlo.at[i], pzhi.at[i]
        )

    def exchange_wide(base, f, zs, cs, lo_x, hi_x, lo_z, hi_z, hold):
        sem = [(side_s.at[base + i], side_r.at[base + i]) for i in range(8)]
        for k, r in enumerate((rows - 1, last, cz_n - 1, 0)):
            cs[k] = f[pl.ds(r, 1), :]
        for k in range(2):
            zs[0, k] = f[pl.ds(cz_n - 2 + k, cx_n, stride=cz_n), :]
            zs[1, k] = f[pl.ds(k, cx_n, stride=cz_n), :]
        copies = [
            send(cs.at[k], hold.at[k], *sem[k], to) for k, to in enumerate(corners)
        ]
        copies.append(send(zs.at[0], lo_z, *sem[4], north))
        copies.append(send(zs.at[1], hi_z, *sem[5], south))
        copies.append(send(f.at[pl.ds(last - cz_n, 2 * cz_n), :], lo_x, *sem[6], east))
        copies.append(send(f.at[pl.ds(0, 2 * cz_n), :], hi_x, *sem[7], west))
        return copies

    def arrive(copies):
        for copy in copies:
            copy.wait_recv()

    level = lax.broadcasted_iota(jnp.int32, (rows, ny), 1)
    depth = lax.rem(lax.broadcasted_iota(jnp.int32, (rows, ny), 0), cz_n)
    bottom = level == 0
    top = level == ny - 1
    front = depth == 0
    back = depth == cz_n - 1

    def spread(edge):
        wide = jnp.broadcast_to(edge[..., None, :], edge.shape[:-1] + (cz_n, ny))
        return wide.reshape(edge.shape[:-2] + (rows, ny))

    def x_prev(f, edge):
        return jnp.concatenate([edge, f[..., : rows - cz_n, :]], -2)

    def x_next(f, edge):
        return jnp.concatenate([f[..., cz_n:, :], edge], -2)

    def z_prev(f, edge):
        return jnp.where(front, spread(edge), pltpu.roll(f, 1, f.ndim - 2))

    def z_next(f, edge):
        return jnp.where(back, spread(edge), pltpu.roll(f, rows - 1, f.ndim - 2))

    def y_prev(f):
        return pltpu.roll(f, 1, f.ndim - 1)

    def y_next(f):
        return pltpu.roll(f, ny - 1, f.ndim - 1)

    halo0 = exchange_field(0, x0_ref)
    coef_send[...] = face_ref[1, pl.ds(cz_n - 1, cx_n, stride=cz_n), :]
    coefs = [
        send(face_ref.at[0, pl.ds(last, cz_n), :], coef_x, coef_ssem.at[0], coef_rsem.at[0], east),
        send(coef_send, coef_z, coef_ssem.at[1], coef_rsem.at[1], north),
    ]
    cy = face_ref[2]
    upper = jnp.where(top, 0.0, cy)
    lower = jnp.where(bottom, 0.0, y_prev(cy))
    wall = jnp.where(bottom | top, jnp.broadcast_to(cy[:, ny - 1 :], (rows, ny)), 0.0)
    cyu[...] = upper
    cyl[...] = lower
    loads[2].wait()
    base = diag_ref[...] + (face_ref[0] + face_ref[1]) + (upper + lower) + wall
    eye = lax.broadcasted_iota(jnp.int32, (cz_n, cz_n), 0) == lax.broadcasted_iota(
        jnp.int32, (cz_n, cz_n), 1
    )

    def column(side):
        flags = bc_ref[side].astype(jnp.float32)
        parts = [
            jnp.sum(
                jnp.where(eye, jnp.broadcast_to(flags[i : i + 1], (cz_n, cz_n)), 0.0),
                axis=1, keepdims=True,
            )
            for i in range(cx_n)
        ]
        return jnp.broadcast_to(jnp.concatenate(parts, 0), (rows, ny))

    arrive(coefs)
    west_c = x_prev(face_ref[0], coef_x[...])
    south_c = z_prev(face_ref[1], coef_z[...])
    cxl[...] = west_c
    czl[...] = south_c
    dgn[...] = base + (west_c + south_c)

    def apply(f, i):
        total = dgn[...] * f
        total -= face_ref[0] * x_next(f, xhi[i]) + cxl[...] * x_prev(f, xlo[i])
        total -= face_ref[1] * z_next(f, zhi[i]) + czl[...] * z_prev(f, zlo[i])
        total -= cyu[...] * y_next(f) + cyl[...] * y_prev(f)
        return total

    def dots(pairs):
        sums = [jnp.sum(a * b, axis=1, keepdims=True) for a, b in pairs]
        while len(sums) < PAD:
            sums.append(jnp.zeros_like(sums[0]))
        stack = jnp.concatenate(sums, 1).reshape(3 * PAD, ny)
        total = jnp.sum(stack, axis=1, keepdims=True)
        shape = (3 * PAD, 128)
        pick = lax.broadcasted_iota(jnp.int32, shape, 0) == lax.broadcasted_iota(
            jnp.int32, shape, 1
        )
        return jnp.sum(
            jnp.where(pick, jnp.broadcast_to(total, shape), 0.0), axis=0, keepdims=True
        )

    def scatter(msg, got, ssem, rsem, others):
        return [
            send(msg, got.at[d], ssem.at[d], rsem, to) for d, to in enumerate(others)
        ]

    def gathered(msg, got, rsem):
        pltpu.make_async_copy(got, got, rsem).wait()
        return msg[...] + jnp.sum(got[...], axis=0)

    def unpack(total):
        shape = (3 * PAD, 128)
        pick = lax.broadcasted_iota(jnp.int32, shape, 0) == lax.broadcasted_iota(
            jnp.int32, shape, 1
        )
        col = jnp.sum(
            jnp.where(pick, jnp.broadcast_to(total, shape), 0.0), axis=1, keepdims=True
        )
        wide = jnp.broadcast_to(col, (3 * PAD, ny)).reshape(3, PAD, ny)
        return [wide[:, k : k + 1] for k in range(PAD)]

    def sums_start(i, pairs):
        msg_x[i] = dots(pairs)
        scatter(msg_x.at[i], got_x.at[i], sum_sx.at[i], sum_rx.at[i], row_x)

    def sums_turn(i):
        msg_z[i] = gathered(msg_x.at[i], got_x.at[i], sum_rx.at[i])
        scatter(msg_z.at[i], got_z.at[i], sum_sz.at[i], sum_rz.at[i], row_z)

    def sums_end(i):
        return unpack(gathered(msg_z.at[i], got_z.at[i], sum_rz.at[i]))

    for load in loads[3:]:
        load.wait()
    arrive(halo0)
    fld[1] = src_ref[...] - apply(x0_ref[...], 0)
    halo = exchange_field(1, fld.at[1])
    pdiag = 6.0 - jnp.where(bottom | top, 1.0, 0.0)
    pdiag = pdiag + jnp.where(bottom, column(0), 0.0) + jnp.where(top, column(1), 0.0)
    share = jacobi_weight / pdiag
    prs[4, 0] = pdiag
    aside = exchange_wide(
        0, map_ref, mzsend, mc_send, mxlo, mxhi, mzlo, mzhi, mc
    )
    aside.append(send(inv_ref, inv_w, side_s.at[16], side_r.at[16], east))
    aside.append(send(inv_ref, inv_e, side_s.at[17], side_r.at[17], west))
    aside += exchange(
        8, prs.at[4], dzsend, dxlo, dxhi, dzlo, dzhi
    )
    arrive(halo)
    fld[2] = apply(fld[1], 1)
    halo = exchange_field(2, fld.at[2])
    arrive(halo)
    fld[3] = apply(fld[2], 2)
    halo = exchange_field(3, fld.at[3])
    r, v, u = fld[1], fld[2], fld[3]
    sums_start(0, [(r, r), (r, v), (r, u), (v, v), (v, u), (u, u)])
    arrive(halo)
    fld[4] = apply(fld[3], 3)
    halo = exchange_field(4, fld.at[4])
    sums_turn(0)
    arrive(halo)
    z = apply(fld[4], 4)
    rr, rv, ru, vv, vu, uu = sums_end(0)[:6]
    alpha = rr / rv
    omega = (rv - alpha * (vv + ru) + alpha * alpha * vu) / (
        vv - 2.0 * alpha * vu + alpha * alpha * uu
    )
    rho_new = (rr - alpha * rv) - omega * (rv - alpha * ru)
    beta = (rho_new / rr) * (alpha / omega)

    def first(x, r, v, u, y, a, w, b):
        s = r - a * v
        t = v - a * u
        x1 = x + a * r + w * s
        r1 = s - w * t
        p2 = r1 + b * (r - w * v)
        mr1 = t - w * (u - a * y)
        v2 = mr1 + b * (v - w * u)
        return x1, r1, p2, v2, mr1

    r, v, u, y = fld[1], fld[2], fld[3], fld[4]
    x1, r1, p2, v2, mr1 = first(x0_ref[...], r, v, u, y, alpha, omega, beta)
    mv2 = (u - alpha * y) - omega * (y - alpha * z) + beta * (u - omega * y)
    sums_start(
        1,
        [(r, v2), (r1, mr1), (r1, mv2), (v2, mr1), (v2, mv2), (mr1, mr1), (mr1, mv2), (mv2, mv2)],
    )
    fld[5] = x1
    fld[6] = r1
    fld[7] = p2
    fld[8] = v2

    def edge_of(buf, c):
        return first(
            *[buf[i, c] for i in range(5)], alpha[c], omega[c], beta[c]
        )[:4]

    edge_x = edge_of(xlo, 0)
    edge_z = edge_of(zlo, 1)
    sums_turn(1)
    rv2, k1, k2, k3, k4, k5, k6, k7 = sums_end(1)
    alpha2 = rho_new / rv2
    omega2 = (k1 - alpha2 * (k2 + k3) + alpha2 * alpha2 * k4) / (
        k5 - 2.0 * alpha2 * k6 + alpha2 * alpha2 * k7
    )

    def second(x1, r1, p2, v2, a, w):
        return x1 + a * p2 + w * (r1 - a * v2)

    velocity = second(fld[5], fld[6], fld[7], fld[8], alpha2, omega2)
    vel_ref[...] = velocity
    west_u = second(*edge_x, alpha2[0], omega2[0])
    south_w = second(*edge_z, alpha2[1], omega2[1])
    ux, uz, uy = velocity[0], velocity[1], velocity[2]
    div = (ux - x_prev(ux, west_u)) + (uz - z_prev(uz, south_w))
    div = div + (uy - jnp.where(bottom, 0.0, y_prev(uy)))

    edge_rows = (cz_n, cz_n, cx_n, cx_n)

    def operate(f, edges):
        near = x_next(f, edges[1]) + x_prev(f, edges[0])
        near += z_next(f, edges[3]) + z_prev(f, edges[2])
        near += jnp.where(top, 0.0, y_next(f)) + jnp.where(bottom, 0.0, y_prev(f))
        return pdiag * f - near

    def at_face(k, f, beyond, inside, before, after):
        n = edge_rows[k]
        pos = lax.broadcasted_iota(jnp.int32, (n, ny), 0)
        lane = lax.broadcasted_iota(jnp.int32, (n, ny), 1)
        near = (beyond + inside) + (
            jnp.where(pos == 0, before, pltpu.roll(f, 1, 0))
            + jnp.where(pos == n - 1, after, pltpu.roll(f, n - 1, 0))
        )
        near += jnp.where(lane == ny - 1, 0.0, y_next(f)) + jnp.where(lane == 0, 0.0, y_prev(f))
        return face_d[k] * f - near

    def insides(ref):
        return (
            ref[pl.ds(0, cz_n), :],
            ref[pl.ds(last, cz_n), :],
            ref[pl.ds(0, cx_n, stride=cz_n), :],
            ref[pl.ds(cz_n - 1, cx_n, stride=cz_n), :],
        )

    around = ((0, 1), (2, 3), (0, 2), (1, 3))

    def operate_faces(ref, near, far, corner):
        return [
            at_face(k, near[k], far[k], inside, corner[around[k][0]], corner[around[k][1]])
            for k, inside in enumerate(insides(ref))
        ]

    def split(lo_x, hi_x, lo_z, hi_z):
        near = (lo_x[cz_n:], hi_x[:cz_n], lo_z[1], hi_z[0])
        far = (lo_x[:cz_n], hi_x[cz_n:], lo_z[0], hi_z[1])
        return near, far

    q = share * div
    qref = prs.at[0, 0]
    qref[...] = q
    wide = exchange_wide(8, qref, qzsend, qc_send, qxlo, qxhi, qzlo, qzhi, qc)
    arrive(aside)
    face_d = (dxlo[0], dxhi[0], dzlo[0], dzhi[0])
    face_share = [jacobi_weight / d for d in face_d]
    arrive(wide)
    near, far = split(qxlo[...], qxhi[...], qzlo[...], qzhi[...])
    edges = [
        2.0 * near[k] - face_share[k] * out
        for k, out in enumerate(operate_faces(qref, near, far, [qc[k] for k in range(4)]))
    ]
    q = 2.0 * q - share * operate(q, near)
    res = div - operate(q, edges)
    cells = map_ref[...]
    parts = [
        jnp.sum(jnp.where(cells == m, res, 0.0), axis=0, keepdims=True) for m in range(COARSE)
    ]
    total = jnp.sum(jnp.concatenate(parts, 0), axis=1, keepdims=True)
    shape = (COARSE, lanes)
    place = lax.broadcasted_iota(jnp.int32, shape, 1) == (
        lax.broadcasted_iota(jnp.int32, shape, 0) + gz * COARSE
    )
    msg_c[...] = jnp.sum(
        jnp.where(place, jnp.broadcast_to(total, shape), 0.0), axis=0, keepdims=True
    )
    side = n_gz - 1
    scatter(msg_c, got_w, coarse_s.at[pl.ds(0, n_gz)], coarse_r.at[0], [east] + aside_e)
    scatter(msg_c, got_e, coarse_s.at[pl.ds(n_gz, n_gz)], coarse_r.at[1], [west] + aside_w)
    scatter(msg_c, got_c, coarse_s.at[pl.ds(2 * n_gz, side)], coarse_r.at[2], row_z)
    q = q + share * res
    prs[1, 0] = q
    halo = exchange_pressure(1)
    arrive(halo)
    q = q + share * (div - operate(q, (pxlo[1, 0], pxhi[1, 0], pzlo[1, 0], pzhi[1, 0])))

    spots = (south[1], gz, north[1])

    def corrections(inv, coarse):
        out = []
        for spot in spots:
            block = inv[pl.ds(pl.multiple_of(spot * COARSE, COARSE), COARSE), :]
            col = jnp.sum(block * coarse[:, : block.shape[1]], axis=1, keepdims=True)
            out.append(jnp.broadcast_to(col, (COARSE, ny)))
        return out

    def lift(cell, corr):
        add = jnp.broadcast_to(corr[0:1], cell.shape)
        for m in range(1, COARSE):
            add = jnp.where(cell == m, corr[m : m + 1], add)
        return add

    def whole(got, rsem):
        pltpu.make_async_copy(got, got, rsem).wait()
        return jnp.sum(got[...], axis=0)

    south_k, own_k, north_k = corrections(inv_ref, gathered(msg_c, got_c, coarse_r.at[2]))
    west_k = corrections(inv_w, whole(got_w, coarse_r.at[0]))
    east_k = corrections(inv_e, whole(got_e, coarse_r.at[1]))
    e = lift(cells, own_k)
    eref = prs.at[2, 0]
    eref[...] = e
    near, far = split(
        lift(mxlo[...], west_k[1]),
        lift(mxhi[...], east_k[1]),
        lift(mzlo[...], south_k),
        lift(mzhi[...], north_k),
    )
    points = [
        lift(mc[k], c) for k, c in enumerate((west_k[0], west_k[2], east_k[0], east_k[2]))
    ]
    edges = [
        near[k] - face_share[k] * out
        for k, out in enumerate(operate_faces(eref, near, far, points))
    ]
    e = e - share * operate(e, near)
    e = e - share * operate(e, edges)
    out_ref[...] = q + e
    for copy in pending:
        copy.wait_send()


def body(n_gx, n_gz, velocity_old, source, diag_coef, face_coef, bc_flags, coarse_map, coarse_inverse):
    cx_n, cz_n, ny = diag_coef.shape
    rows = cx_n * cz_n
    group = coarse_inverse.shape[1]
    lanes = -(-group // 128) * 128
    f32 = jnp.float32
    vmem = pltpu.VMEM
    dma = pltpu.SemaphoreType.DMA

    def wide_set(kind):
        return [
            vmem((2 * cz_n, ny), kind),
            vmem((2 * cz_n, ny), kind),
            vmem((2, cx_n, ny), kind),
            vmem((2, cx_n, ny), kind),
            vmem((2, 2, cx_n, ny), kind),
            vmem((4, 1, ny), kind),
            vmem((4, 1, ny), kind),
        ]

    scratch = [
        vmem((3, rows, ny), f32),
        vmem((3, rows, ny), f32),
        vmem((rows, ny), f32),
        vmem((3, rows, ny), f32),
        vmem(bc_flags.shape, jnp.int32),
        vmem((rows, ny), jnp.int32),
        vmem(coarse_inverse.shape, f32),
        vmem((9, 3, rows, ny), f32),
        vmem((5, 3, cz_n, ny), f32),
        vmem((5, 3, cz_n, ny), f32),
        vmem((5, 3, cx_n, ny), f32),
        vmem((5, 3, cx_n, ny), f32),
        vmem((5, 2, 3, cx_n, ny), f32),
        vmem((cx_n, ny), f32),
        vmem((cz_n, ny), f32),
        vmem((cx_n, ny), f32),
        vmem((5, 1, rows, ny), f32),
        vmem((2, 1, cz_n, ny), f32),
        vmem((2, 1, cz_n, ny), f32),
        vmem((2, 1, cx_n, ny), f32),
        vmem((2, 1, cx_n, ny), f32),
        vmem((2, 2, 1, cx_n, ny), f32),
        *wide_set(f32),
        *wide_set(jnp.int32),
        vmem((1, cz_n, ny), f32),
        vmem((1, cz_n, ny), f32),
        vmem((1, cx_n, ny), f32),
        vmem((1, cx_n, ny), f32),
        vmem((2, 1, cx_n, ny), f32),
        vmem(coarse_inverse.shape, f32),
        vmem(coarse_inverse.shape, f32),
        vmem((rows, ny), f32),
        vmem((rows, ny), f32),
        vmem((rows, ny), f32),
        vmem((rows, ny), f32),
        vmem((rows, ny), f32),
        vmem((2, 1, 128), f32),
        vmem((2, n_gx - 1, 1, 128), f32),
        vmem((2, 1, 128), f32),
        vmem((2, n_gz - 1, 1, 128), f32),
        vmem((1, lanes), f32),
        vmem((n_gz - 1, 1, lanes), f32),
        vmem((n_gz, 1, lanes), f32),
        vmem((n_gz, 1, lanes), f32),
        dma((9, 4)),
        dma((9, 4)),
        dma((2,)),
        dma((2,)),
        dma((2, n_gx - 1)),
        dma((2,)),
        dma((2, n_gz - 1)),
        dma((2,)),
        dma((3 * n_gz - 1,)),
        dma((3,)),
        dma((7,)),
        dma((18,)),
        dma((18,)),
    ]
    spec = pl.BlockSpec(memory_space=pltpu.VMEM)
    velocity, pressure = pl.pallas_call(
        functools.partial(kernel, (n_gx, n_gz, cx_n, cz_n, ny, lanes)),
        out_shape=(
            jax.ShapeDtypeStruct((3, rows, ny), f32),
            jax.ShapeDtypeStruct((rows, ny), f32),
        ),
        in_specs=[pl.BlockSpec(memory_space=pltpu.HBM)] * 7,
        out_specs=(spec, spec),
        scratch_shapes=scratch,
        compiler_params=pltpu.CompilerParams(
            collective_id=0, has_side_effects=True
        ),
        name="corrector",
    )(
        velocity_old.reshape(3, rows, ny),
        source.reshape(3, rows, ny),
        diag_coef.reshape(rows, ny),
        face_coef.reshape(3, rows, ny),
        bc_flags,
        coarse_map.reshape(rows, ny),
        coarse_inverse,
    )
    return velocity.reshape(3, cx_n, cz_n, ny), pressure.reshape(cx_n, cz_n, ny)


def solution(mesh):
    placed = (
        P(None, "gx", "gz", None),
        P(None, "gx", "gz", None),
        P("gx", "gz", None),
        P(None, "gx", "gz", None),
        P(None, "gx", "gz"),
        P("gx", "gz", None),
        P("gx", None),
    )
    return jax.shard_map(
        functools.partial(body, mesh.shape["gx"], mesh.shape["gz"]),
        mesh=mesh,
        in_specs=placed,
        out_specs=(P(None, "gx", "gz", None), P("gx", "gz", None)),
        check_vma=False,
    )
```

```python
import functools

import jax
import jax.numpy as jnp
from jax import lax
from jax.experimental import pallas as pl
from jax.experimental.pallas import tpu as pltpu
from jax.sharding import PartitionSpec as P

COARSE = 16
PAD = 8

jacobi_weight = 2.0 / 3.0
MESH = pl.DeviceIdType.MESH


def kernel(
    dims,
    x0_in, src_in, diag_in, face_in, bc_in, map_in, inv_in,
    vel_ref, out_ref,
    x0_ref, src_ref, diag_ref, face_ref, bc_ref, map_ref, inv_ref,
    fld, xlo, xhi, zlo, zhi, zsend,
    wxlo, wxhi, wzlo, wzhi, wzsend, wc_send, wc,
    coef_send, coef_x, coef_z,
    prs, pxlo, pxhi, pzlo, pzhi, pzsend,
    qxlo, qxhi, qzlo, qzhi, qzsend, qc_send, qc,
    mxlo, mxhi, mzlo, mzhi, mzsend, mc_send, mc,
    dxlo, dxhi, dzlo, dzhi, dzsend, inv_w, inv_e,
    coef, kxlo, kxhi, kzlo, kzhi, kzsend,
    msg_x, got_x, msg_z, got_z, msg_c, got_c, got_w, got_e,
    send_sem, recv_sem, coef_ssem, coef_rsem,
    sum_sx, sum_rx, sum_sz, sum_rz, coarse_s, coarse_r,
    load_sem, side_s, side_r,
):
    n_gx, n_gz, cx_n, cz_n, ny, lanes = dims
    rows = cx_n * cz_n
    gx = lax.axis_index("gx")
    gz = lax.axis_index("gz")
    east = (lax.rem(gx + 1, n_gx), gz)
    west = (lax.rem(gx + n_gx - 1, n_gx), gz)
    north = (gx, lax.rem(gz + 1, n_gz))
    south = (gx, lax.rem(gz + n_gz - 1, n_gz))
    row_x = [(lax.rem(gx + d, n_gx), gz) for d in range(1, n_gx)]
    row_z = [(gx, lax.rem(gz + d, n_gz)) for d in range(1, n_gz)]
    pending = []

    def send(src, dst, ssem, rsem, to):
        copy = pltpu.make_async_remote_copy(
            src_ref=src, dst_ref=dst, send_sem=ssem, recv_sem=rsem,
            device_id=to, device_id_type=MESH,
        )
        copy.start()
        pending.append(copy)
        return copy

    aside_w = [(west[0], to[1]) for to in row_z]
    aside_e = [(east[0], to[1]) for to in row_z]
    corners = [
        (east[0], north[1]), (east[0], south[1]), (west[0], north[1]), (west[0], south[1])
    ]
    loads = [
        pltpu.make_async_copy(a, b, load_sem.at[i])
        for i, (a, b) in enumerate(
            [
                (x0_in, x0_ref), (face_in, face_ref), (diag_in, diag_ref), (src_in, src_ref),
                (bc_in, bc_ref), (map_in, map_ref), (inv_in, inv_ref),
            ]
        )
    ]
    for load in loads:
        load.start()
    barrier = pltpu.get_barrier_semaphore()
    partners = row_x + row_z + aside_w + aside_e
    for other in partners:
        pl.semaphore_signal(barrier, inc=1, device_id=other, device_id_type=MESH)
    loads[0].wait()
    loads[1].wait()
    pl.semaphore_wait(barrier, len(partners))

    last = rows - cz_n

    def exchange(phase, src, zs, lo_x, hi_x, lo_z, hi_z):
        zs[0] = src[:, pl.ds(cz_n - 1, cx_n, stride=cz_n), :]
        zs[1] = src[:, pl.ds(0, cx_n, stride=cz_n), :]
        sems = [(send_sem.at[phase, i], recv_sem.at[phase, i]) for i in range(4)]
        return [
            send(zs.at[0], lo_z, *sems[2], north),
            send(zs.at[1], hi_z, *sems[3], south),
            send(src.at[:, pl.ds(last, cz_n), :], lo_x, *sems[0], east),
            send(src.at[:, pl.ds(0, cz_n), :], hi_x, *sems[1], west),
        ]

    def exchange_pressure(i):
        return exchange(
            5 + i, prs.at[i], pzsend.at[i], pxlo.at[i], pxhi.at[i], pzlo.at[i], pzhi.at[i]
        )

    def part(ref, which):
        return (slice(None),) * (len(ref.shape) - 2) + (which, slice(None))

    def exchange_wide(base, f, zs, cs, lo_x, hi_x, lo_z, hi_z, hold):
        sem = [(side_s.at[base + i], side_r.at[base + i]) for i in range(8)]
        for k, r in enumerate((rows - 1, last, cz_n - 1, 0)):
            cs[k] = f[part(f, pl.ds(r, 1))]
        for k in range(2):
            zs[0, k] = f[part(f, pl.ds(cz_n - 2 + k, cx_n, stride=cz_n))]
            zs[1, k] = f[part(f, pl.ds(k, cx_n, stride=cz_n))]
        copies = [
            send(cs.at[k], hold.at[k], *sem[k], to) for k, to in enumerate(corners)
        ]
        copies.append(send(zs.at[0], lo_z, *sem[4], north))
        copies.append(send(zs.at[1], hi_z, *sem[5], south))
        copies.append(send(f.at[part(f, pl.ds(last - cz_n, 2 * cz_n))], lo_x, *sem[6], east))
        copies.append(send(f.at[part(f, pl.ds(0, 2 * cz_n))], hi_x, *sem[7], west))
        return copies

    def arrive(copies):
        for copy in copies:
            copy.wait_recv()

    level = lax.broadcasted_iota(jnp.int32, (rows, ny), 1)
    depth = lax.rem(lax.broadcasted_iota(jnp.int32, (rows, ny), 0), cz_n)
    bottom = level == 0
    top = level == ny - 1
    front = depth == 0
    back = depth == cz_n - 1

    def spread(edge):
        wide = jnp.broadcast_to(edge[..., None, :], edge.shape[:-1] + (cz_n, ny))
        return wide.reshape(edge.shape[:-2] + (rows, ny))

    def x_prev(f, edge):
        return jnp.concatenate([edge, f[..., : rows - cz_n, :]], -2)

    def x_next(f, edge):
        return jnp.concatenate([f[..., cz_n:, :], edge], -2)

    def z_prev(f, edge):
        return jnp.where(front, spread(edge), pltpu.roll(f, 1, f.ndim - 2))

    def z_next(f, edge):
        return jnp.where(back, spread(edge), pltpu.roll(f, rows - 1, f.ndim - 2))

    def y_prev(f):
        return pltpu.roll(f, 1, f.ndim - 1)

    def y_next(f):
        return pltpu.roll(f, ny - 1, f.ndim - 1)

    halo0 = exchange(0, x0_ref, zsend, xlo, xhi, zlo, zhi)
    coef_send[...] = face_ref[1, pl.ds(cz_n - 1, cx_n, stride=cz_n), :]
    coefs = [
        send(face_ref.at[0, pl.ds(last, cz_n), :], coef_x, coef_ssem.at[0], coef_rsem.at[0], east),
        send(coef_send, coef_z, coef_ssem.at[1], coef_rsem.at[1], north),
    ]
    cy = face_ref[2]
    upper = jnp.where(top, 0.0, cy)
    lower = jnp.where(bottom, 0.0, y_prev(cy))
    wall = jnp.where(bottom | top, jnp.broadcast_to(cy[:, ny - 1 :], (rows, ny)), 0.0)
    coef[1] = face_ref[0]
    coef[3] = face_ref[1]
    coef[5] = upper
    coef[6] = lower
    loads[2].wait()
    base = diag_ref[...] + (face_ref[0] + face_ref[1]) + (upper + lower) + wall
    eye = lax.broadcasted_iota(jnp.int32, (cz_n, cz_n), 0) == lax.broadcasted_iota(
        jnp.int32, (cz_n, cz_n), 1
    )

    def column(side):
        flags = bc_ref[side].astype(jnp.float32)
        parts = [
            jnp.sum(
                jnp.where(eye, jnp.broadcast_to(flags[i : i + 1], (cz_n, cz_n)), 0.0),
                axis=1, keepdims=True,
            )
            for i in range(cx_n)
        ]
        return jnp.broadcast_to(jnp.concatenate(parts, 0), (rows, ny))

    arrive(coefs)
    west_c = x_prev(face_ref[0], coef_x[...])
    south_c = z_prev(face_ref[1], coef_z[...])
    coef[2] = west_c
    coef[4] = south_c
    coef[0] = base + (west_c + south_c)

    def apply(f, edges):
        total = coef[0] * f
        total -= coef[1] * x_next(f, edges[1]) + coef[2] * x_prev(f, edges[0])
        total -= coef[3] * z_next(f, edges[3]) + coef[4] * z_prev(f, edges[2])
        total -= coef[5] * y_next(f) + coef[6] * y_prev(f)
        return total

    edge_rows = (cz_n, cz_n, cx_n, cx_n)
    around = ((0, 1), (2, 3), (0, 2), (1, 3))

    def insides(ref):
        return (
            ref[part(ref, pl.ds(0, cz_n))],
            ref[part(ref, pl.ds(last, cz_n))],
            ref[part(ref, pl.ds(0, cx_n, stride=cz_n))],
            ref[part(ref, pl.ds(cz_n - 1, cx_n, stride=cz_n))],
        )

    def split(lo_x, hi_x, lo_z, hi_z):
        near = (lo_x[..., cz_n:, :], hi_x[..., :cz_n, :], lo_z[1], hi_z[0])
        far = (lo_x[..., :cz_n, :], hi_x[..., cz_n:, :], lo_z[0], hi_z[1])
        return near, far

    def along_face(k, f, before, after):
        n = edge_rows[k]
        pos = lax.broadcasted_iota(jnp.int32, (n, ny), 0)
        return (
            jnp.where(pos == 0, before, pltpu.roll(f, 1, f.ndim - 2)),
            jnp.where(pos == n - 1, after, pltpu.roll(f, n - 1, f.ndim - 2)),
        )

    face_coefs = (kxlo, kxhi, kzlo, kzhi)

    def apply_faces(ref, near, far, corner):
        out = []
        for k, inside in enumerate(insides(ref)):
            f, c = near[k], face_coefs[k]
            down, up = (far[k], inside) if k % 2 == 0 else (inside, far[k])
            before, after = along_face(k, f, corner[around[k][0]], corner[around[k][1]])
            n, t = (1, 3) if k < 2 else (3, 1)
            total = c[0] * f
            total -= c[n] * up + c[n + 1] * down
            total -= c[t] * after + c[t + 1] * before
            total -= c[5] * y_next(f) + c[6] * y_prev(f)
            out.append(total)
        return out

    def wide_field(i, ref):
        return exchange_wide(
            18 + 8 * i, ref, wzsend.at[i], wc_send.at[i],
            wxlo.at[i], wxhi.at[i], wzlo.at[i], wzhi.at[i], wc.at[i],
        )

    def wide_edges(i):
        near, far = split(wxlo[i], wxhi[i], wzlo[i], wzhi[i])
        return near, far, [wc[i, k] for k in range(4)]

    def dots(pairs):
        sums = [jnp.sum(a * b, axis=1, keepdims=True) for a, b in pairs]
        while len(sums) < PAD:
            sums.append(jnp.zeros_like(sums[0]))
        stack = jnp.concatenate(sums, 1).reshape(3 * PAD, ny)
        total = jnp.sum(stack, axis=1, keepdims=True)
        shape = (3 * PAD, 128)
        pick = lax.broadcasted_iota(jnp.int32, shape, 0) == lax.broadcasted_iota(
            jnp.int32, shape, 1
        )
        return jnp.sum(
            jnp.where(pick, jnp.broadcast_to(total, shape), 0.0), axis=0, keepdims=True
        )

    def scatter(msg, got, ssem, rsem, others):
        return [
            send(msg, got.at[d], ssem.at[d], rsem, to) for d, to in enumerate(others)
        ]

    def gathered(msg, got, rsem):
        pltpu.make_async_copy(got, got, rsem).wait()
        return msg[...] + jnp.sum(got[...], axis=0)

    def unpack(total):
        shape = (3 * PAD, 128)
        pick = lax.broadcasted_iota(jnp.int32, shape, 0) == lax.broadcasted_iota(
            jnp.int32, shape, 1
        )
        col = jnp.sum(
            jnp.where(pick, jnp.broadcast_to(total, shape), 0.0), axis=1, keepdims=True
        )
        wide = jnp.broadcast_to(col, (3 * PAD, ny)).reshape(3, PAD, ny)
        return [wide[:, k : k + 1] for k in range(PAD)]

    def sums_start(i, pairs):
        msg_x[i] = dots(pairs)
        scatter(msg_x.at[i], got_x.at[i], sum_sx.at[i], sum_rx.at[i], row_x)

    def sums_turn(i):
        msg_z[i] = gathered(msg_x.at[i], got_x.at[i], sum_rx.at[i])
        scatter(msg_z.at[i], got_z.at[i], sum_sz.at[i], sum_rz.at[i], row_z)

    def sums_end(i):
        return unpack(gathered(msg_z.at[i], got_z.at[i], sum_rz.at[i]))

    for load in loads[3:]:
        load.wait()
    arrive(halo0)
    fld[1] = src_ref[...] - apply(x0_ref[...], (xlo[...], xhi[...], zlo[...], zhi[...]))
    wide = wide_field(0, fld.at[1])
    aside = exchange(1, coef, kzsend, kxlo, kxhi, kzlo, kzhi)
    pdiag = 6.0 - jnp.where(bottom | top, 1.0, 0.0)
    pdiag = pdiag + jnp.where(bottom, column(0), 0.0) + jnp.where(top, column(1), 0.0)
    share = jacobi_weight / pdiag
    prs[4, 0] = pdiag
    arrive(wide)
    r_near, r_far, r_corner = wide_edges(0)
    v = apply(fld[1], r_near)
    fld[2] = v
    arrive(aside)
    v_near = apply_faces(fld.at[1], r_near, r_far, r_corner)
    fld[3] = apply(v, v_near)
    wide = wide_field(1, fld.at[3])
    r, v, u = fld[1], fld[2], fld[3]
    sums_start(0, [(r, r), (r, v), (r, u), (v, v), (v, u), (u, u)])
    aside = exchange_wide(
        0, map_ref, mzsend, mc_send, mxlo, mxhi, mzlo, mzhi, mc
    )
    aside.append(send(inv_ref, inv_w, side_s.at[16], side_r.at[16], east))
    aside.append(send(inv_ref, inv_e, side_s.at[17], side_r.at[17], west))
    aside += exchange(
        8, prs.at[4], dzsend, dxlo, dxhi, dzlo, dzhi
    )
    sums_turn(0)
    arrive(wide)
    u_near, u_far, u_corner = wide_edges(1)
    y = apply(fld[3], u_near)
    fld[4] = y
    y_near = apply_faces(fld.at[3], u_near, u_far, u_corner)
    z = apply(y, y_near)
    rr, rv, ru, vv, vu, uu = sums_end(0)[:6]
    alpha = rr / rv
    omega = (rv - alpha * (vv + ru) + alpha * alpha * vu) / (
        vv - 2.0 * alpha * vu + alpha * alpha * uu
    )
    rho_new = (rr - alpha * rv) - omega * (rv - alpha * ru)
    beta = (rho_new / rr) * (alpha / omega)

    def first(x, r, v, u, y, a, w, b):
        s = r - a * v
        t = v - a * u
        x1 = x + a * r + w * s
        r1 = s - w * t
        p2 = r1 + b * (r - w * v)
        mr1 = t - w * (u - a * y)
        v2 = mr1 + b * (v - w * u)
        return x1, r1, p2, v2, mr1

    r, v, u, y = fld[1], fld[2], fld[3], fld[4]
    x1, r1, p2, v2, mr1 = first(x0_ref[...], r, v, u, y, alpha, omega, beta)
    mv2 = (u - alpha * y) - omega * (y - alpha * z) + beta * (u - omega * y)
    sums_start(
        1,
        [(r, v2), (r1, mr1), (r1, mv2), (v2, mr1), (v2, mv2), (mr1, mr1), (mr1, mv2), (mv2, mv2)],
    )
    fld[5] = x1
    fld[6] = r1
    fld[7] = p2
    fld[8] = v2

    def edge_of(k, c):
        start = (xlo, xhi, zlo, zhi)[k]
        return first(
            start[c], r_near[k][c], v_near[k][c], u_near[k][c], y_near[k][c],
            alpha[c], omega[c], beta[c],
        )[:4]

    edge_x = edge_of(0, 0)
    edge_z = edge_of(2, 1)
    sums_turn(1)
    rv2, k1, k2, k3, k4, k5, k6, k7 = sums_end(1)
    alpha2 = rho_new / rv2
    omega2 = (k1 - alpha2 * (k2 + k3) + alpha2 * alpha2 * k4) / (
        k5 - 2.0 * alpha2 * k6 + alpha2 * alpha2 * k7
    )

    def second(x1, r1, p2, v2, a, w):
        return x1 + a * p2 + w * (r1 - a * v2)

    velocity = second(fld[5], fld[6], fld[7], fld[8], alpha2, omega2)
    vel_ref[...] = velocity
    west_u = second(*edge_x, alpha2[0], omega2[0])
    south_w = second(*edge_z, alpha2[1], omega2[1])
    ux, uz, uy = velocity[0], velocity[1], velocity[2]
    div = (ux - x_prev(ux, west_u)) + (uz - z_prev(uz, south_w))
    div = div + (uy - jnp.where(bottom, 0.0, y_prev(uy)))

    def operate(f, edges):
        near = x_next(f, edges[1]) + x_prev(f, edges[0])
        near += z_next(f, edges[3]) + z_prev(f, edges[2])
        near += jnp.where(top, 0.0, y_next(f)) + jnp.where(bottom, 0.0, y_prev(f))
        return pdiag * f - near

    def at_face(k, f, beyond, inside, before, after):
        lane = lax.broadcasted_iota(jnp.int32, f.shape, 1)
        before, after = along_face(k, f, before, after)
        near = (beyond + inside) + (before + after)
        near += jnp.where(lane == ny - 1, 0.0, y_next(f)) + jnp.where(lane == 0, 0.0, y_prev(f))
        return face_d[k] * f - near

    def operate_faces(ref, near, far, corner):
        return [
            at_face(k, near[k], far[k], inside, corner[around[k][0]], corner[around[k][1]])
            for k, inside in enumerate(insides(ref))
        ]

    q = share * div
    qref = prs.at[0, 0]
    qref[...] = q
    wide = exchange_wide(8, qref, qzsend, qc_send, qxlo, qxhi, qzlo, qzhi, qc)
    arrive(aside)
    face_d = (dxlo[0], dxhi[0], dzlo[0], dzhi[0])
    face_share = [jacobi_weight / d for d in face_d]
    arrive(wide)
    near, far = split(qxlo[...], qxhi[...], qzlo[...], qzhi[...])
    edges = [
        2.0 * near[k] - face_share[k] * out
        for k, out in enumerate(operate_faces(qref, near, far, [qc[k] for k in range(4)]))
    ]
    q = 2.0 * q - share * operate(q, near)
    res = div - operate(q, edges)
    cells = map_ref[...]
    parts = [
        jnp.sum(jnp.where(cells == m, res, 0.0), axis=0, keepdims=True) for m in range(COARSE)
    ]
    total = jnp.sum(jnp.concatenate(parts, 0), axis=1, keepdims=True)
    shape = (COARSE, lanes)
    place = lax.broadcasted_iota(jnp.int32, shape, 1) == (
        lax.broadcasted_iota(jnp.int32, shape, 0) + gz * COARSE
    )
    msg_c[...] = jnp.sum(
        jnp.where(place, jnp.broadcast_to(total, shape), 0.0), axis=0, keepdims=True
    )
    side = n_gz - 1
    scatter(msg_c, got_w, coarse_s.at[pl.ds(0, n_gz)], coarse_r.at[0], [east] + aside_e)
    scatter(msg_c, got_e, coarse_s.at[pl.ds(n_gz, n_gz)], coarse_r.at[1], [west] + aside_w)
    scatter(msg_c, got_c, coarse_s.at[pl.ds(2 * n_gz, side)], coarse_r.at[2], row_z)
    q = q + share * res
    prs[1, 0] = q
    halo = exchange_pressure(1)
    arrive(halo)
    q = q + share * (div - operate(q, (pxlo[1, 0], pxhi[1, 0], pzlo[1, 0], pzhi[1, 0])))

    spots = (south[1], gz, north[1])

    def corrections(inv, coarse):
        out = []
        for spot in spots:
            block = inv[pl.ds(pl.multiple_of(spot * COARSE, COARSE), COARSE), :]
            col = jnp.sum(block * coarse[:, : block.shape[1]], axis=1, keepdims=True)
            out.append(jnp.broadcast_to(col, (COARSE, ny)))
        return out

    def lift(cell, corr):
        add = jnp.broadcast_to(corr[0:1], cell.shape)
        for m in range(1, COARSE):
            add = jnp.where(cell == m, corr[m : m + 1], add)
        return add

    def whole(got, rsem):
        pltpu.make_async_copy(got, got, rsem).wait()
        return jnp.sum(got[...], axis=0)

    south_k, own_k, north_k = corrections(inv_ref, gathered(msg_c, got_c, coarse_r.at[2]))
    west_k = corrections(inv_w, whole(got_w, coarse_r.at[0]))
    east_k = corrections(inv_e, whole(got_e, coarse_r.at[1]))
    e = lift(cells, own_k)
    eref = prs.at[2, 0]
    eref[...] = e
    near, far = split(
        lift(mxlo[...], west_k[1]),
        lift(mxhi[...], east_k[1]),
        lift(mzlo[...], south_k),
        lift(mzhi[...], north_k),
    )
    points = [
        lift(mc[k], c) for k, c in enumerate((west_k[0], west_k[2], east_k[0], east_k[2]))
    ]
    edges = [
        near[k] - face_share[k] * out
        for k, out in enumerate(operate_faces(eref, near, far, points))
    ]
    e = e - share * operate(e, near)
    e = e - share * operate(e, edges)
    out_ref[...] = q + e
    for copy in pending:
        copy.wait_send()


def body(n_gx, n_gz, velocity_old, source, diag_coef, face_coef, bc_flags, coarse_map, coarse_inverse):
    cx_n, cz_n, ny = diag_coef.shape
    rows = cx_n * cz_n
    group = coarse_inverse.shape[1]
    lanes = -(-group // 128) * 128
    f32 = jnp.float32
    vmem = pltpu.VMEM
    dma = pltpu.SemaphoreType.DMA

    def wide_set(kind):
        return [
            vmem((2 * cz_n, ny), kind),
            vmem((2 * cz_n, ny), kind),
            vmem((2, cx_n, ny), kind),
            vmem((2, cx_n, ny), kind),
            vmem((2, 2, cx_n, ny), kind),
            vmem((4, 1, ny), kind),
            vmem((4, 1, ny), kind),
        ]

    scratch = [
        vmem((3, rows, ny), f32),
        vmem((3, rows, ny), f32),
        vmem((rows, ny), f32),
        vmem((3, rows, ny), f32),
        vmem(bc_flags.shape, jnp.int32),
        vmem((rows, ny), jnp.int32),
        vmem(coarse_inverse.shape, f32),
        vmem((9, 3, rows, ny), f32),
        vmem((3, cz_n, ny), f32),
        vmem((3, cz_n, ny), f32),
        vmem((3, cx_n, ny), f32),
        vmem((3, cx_n, ny), f32),
        vmem((2, 3, cx_n, ny), f32),
        vmem((2, 3, 2 * cz_n, ny), f32),
        vmem((2, 3, 2 * cz_n, ny), f32),
        vmem((2, 2, 3, cx_n, ny), f32),
        vmem((2, 2, 3, cx_n, ny), f32),
        vmem((2, 2, 2, 3, cx_n, ny), f32),
        vmem((2, 4, 3, 1, ny), f32),
        vmem((2, 4, 3, 1, ny), f32),
        vmem((cx_n, ny), f32),
        vmem((cz_n, ny), f32),
        vmem((cx_n, ny), f32),
        vmem((5, 1, rows, ny), f32),
        vmem((2, 1, cz_n, ny), f32),
        vmem((2, 1, cz_n, ny), f32),
        vmem((2, 1, cx_n, ny), f32),
        vmem((2, 1, cx_n, ny), f32),
        vmem((2, 2, 1, cx_n, ny), f32),
        *wide_set(f32),
        *wide_set(jnp.int32),
        vmem((1, cz_n, ny), f32),
        vmem((1, cz_n, ny), f32),
        vmem((1, cx_n, ny), f32),
        vmem((1, cx_n, ny), f32),
        vmem((2, 1, cx_n, ny), f32),
        vmem(coarse_inverse.shape, f32),
        vmem(coarse_inverse.shape, f32),
        vmem((7, rows, ny), f32),
        vmem((7, cz_n, ny), f32),
        vmem((7, cz_n, ny), f32),
        vmem((7, cx_n, ny), f32),
        vmem((7, cx_n, ny), f32),
        vmem((2, 7, cx_n, ny), f32),
        vmem((2, 1, 128), f32),
        vmem((2, n_gx - 1, 1, 128), f32),
        vmem((2, 1, 128), f32),
        vmem((2, n_gz - 1, 1, 128), f32),
        vmem((1, lanes), f32),
        vmem((n_gz - 1, 1, lanes), f32),
        vmem((n_gz, 1, lanes), f32),
        vmem((n_gz, 1, lanes), f32),
        dma((9, 4)),
        dma((9, 4)),
        dma((2,)),
        dma((2,)),
        dma((2, n_gx - 1)),
        dma((2,)),
        dma((2, n_gz - 1)),
        dma((2,)),
        dma((3 * n_gz - 1,)),
        dma((3,)),
        dma((7,)),
        dma((34,)),
        dma((34,)),
    ]
    spec = pl.BlockSpec(memory_space=pltpu.VMEM)
    velocity, pressure = pl.pallas_call(
        functools.partial(kernel, (n_gx, n_gz, cx_n, cz_n, ny, lanes)),
        out_shape=(
            jax.ShapeDtypeStruct((3, rows, ny), f32),
            jax.ShapeDtypeStruct((rows, ny), f32),
        ),
        in_specs=[pl.BlockSpec(memory_space=pltpu.HBM)] * 7,
        out_specs=(spec, spec),
        scratch_shapes=scratch,
        compiler_params=pltpu.CompilerParams(
            collective_id=0, has_side_effects=True, vmem_limit_bytes=48 * 1024 * 1024
        ),
        name="corrector",
    )(
        velocity_old.reshape(3, rows, ny),
        source.reshape(3, rows, ny),
        diag_coef.reshape(rows, ny),
        face_coef.reshape(3, rows, ny),
        bc_flags,
        coarse_map.reshape(rows, ny),
        coarse_inverse,
    )
    return velocity.reshape(3, cx_n, cz_n, ny), pressure.reshape(cx_n, cz_n, ny)


def solution(mesh):
    placed = (
        P(None, "gx", "gz", None),
        P(None, "gx", "gz", None),
        P("gx", "gz", None),
        P(None, "gx", "gz", None),
        P(None, "gx", "gz"),
        P("gx", "gz", None),
        P("gx", None),
    )
    return jax.shard_map(
        functools.partial(body, mesh.shape["gx"], mesh.shape["gz"]),
        mesh=mesh,
        in_specs=placed,
        out_specs=(P(None, "gx", "gz", None), P("gx", "gz", None)),
        check_vma=False,
    )
```

```python
import functools

import jax
import jax.numpy as jnp
from jax import lax
from jax.experimental import pallas as pl
from jax.experimental.pallas import tpu as pltpu
from jax.sharding import PartitionSpec as P

COARSE = 16
PAD = 8

jacobi_weight = 2.0 / 3.0
MESH = pl.DeviceIdType.MESH


def kernel(
    dims,
    x0_in, src_in, diag_in, face_in, bc_in, map_in, inv_in,
    vel_a, vel_b, prs_a, prs_b,
    x0_ref, src_ref, diag_ref, face_ref, bc_ref, map_ref, inv_ref,
    fld, xlo, xhi, zlo, zhi, zsend,
    wxlo, wxhi, wzlo, wzhi, wzsend, wc_send, wc,
    coef_send, coef_x, coef_z,
    prs, pxlo, pxhi, pzlo, pzhi, pzsend,
    qxlo, qxhi, qzlo, qzhi, qzsend, qc_send, qc,
    mxlo, mxhi, mzlo, mzhi, mzsend, mc_send, mc,
    dxlo, dxhi, dzlo, dzhi, dzsend, inv_w, inv_e,
    coef, kxlo, kxhi, kzlo, kzhi, kzsend,
    msg_x, got_x, msg_z, got_z, msg_c, got_c, got_w, got_e,
    send_sem, recv_sem, coef_ssem, coef_rsem,
    sum_sx, sum_rx, sum_sz, sum_rz, coarse_s, coarse_r,
    load_sem, side_s, side_r, store_sem,
):
    n_gx, n_gz, cx_n, cz_n, ny, lanes = dims
    rows = cx_n * cz_n
    gx = lax.axis_index("gx")
    gz = lax.axis_index("gz")
    east = (lax.rem(gx + 1, n_gx), gz)
    west = (lax.rem(gx + n_gx - 1, n_gx), gz)
    north = (gx, lax.rem(gz + 1, n_gz))
    south = (gx, lax.rem(gz + n_gz - 1, n_gz))
    row_x = [(lax.rem(gx + d, n_gx), gz) for d in range(1, n_gx)]
    row_z = [(gx, lax.rem(gz + d, n_gz)) for d in range(1, n_gz)]
    pending = []

    def send(src, dst, ssem, rsem, to):
        copy = pltpu.make_async_remote_copy(
            src_ref=src, dst_ref=dst, send_sem=ssem, recv_sem=rsem,
            device_id=to, device_id_type=MESH,
        )
        copy.start()
        pending.append(copy)
        return copy

    aside_w = [(west[0], to[1]) for to in row_z]
    aside_e = [(east[0], to[1]) for to in row_z]
    corners = [
        (east[0], north[1]), (east[0], south[1]), (west[0], north[1]), (west[0], south[1])
    ]
    loads = [
        pltpu.make_async_copy(a, b, load_sem.at[i])
        for i, (a, b) in enumerate(
            [
                (x0_in, x0_ref), (face_in, face_ref), (diag_in, diag_ref), (src_in, src_ref),
                (bc_in, bc_ref), (map_in, map_ref), (inv_in, inv_ref),
            ]
        )
    ]
    for load in loads:
        load.start()
    barrier = pltpu.get_barrier_semaphore()
    partners = row_x + row_z + aside_w + aside_e
    for other in partners:
        pl.semaphore_signal(barrier, inc=1, device_id=other, device_id_type=MESH)
    loads[0].wait()
    loads[1].wait()
    pl.semaphore_wait(barrier, len(partners))

    last = rows - cz_n

    def exchange(phase, src, zs, lo_x, hi_x, lo_z, hi_z):
        zs[0] = src[:, pl.ds(cz_n - 1, cx_n, stride=cz_n), :]
        zs[1] = src[:, pl.ds(0, cx_n, stride=cz_n), :]
        sems = [(send_sem.at[phase, i], recv_sem.at[phase, i]) for i in range(4)]
        return [
            send(zs.at[0], lo_z, *sems[2], north),
            send(zs.at[1], hi_z, *sems[3], south),
            send(src.at[:, pl.ds(last, cz_n), :], lo_x, *sems[0], east),
            send(src.at[:, pl.ds(0, cz_n), :], hi_x, *sems[1], west),
        ]

    def exchange_pressure(i):
        return exchange(
            5 + i, prs.at[i], pzsend.at[i], pxlo.at[i], pxhi.at[i], pzlo.at[i], pzhi.at[i]
        )

    def part(ref, which):
        return (slice(None),) * (len(ref.shape) - 2) + (which, slice(None))

    def exchange_wide(base, f, zs, cs, lo_x, hi_x, lo_z, hi_z, hold):
        sem = [(side_s.at[base + i], side_r.at[base + i]) for i in range(8)]
        for k, r in enumerate((rows - 1, last, cz_n - 1, 0)):
            cs[k] = f[part(f, pl.ds(r, 1))]
        for k in range(2):
            zs[0, k] = f[part(f, pl.ds(cz_n - 2 + k, cx_n, stride=cz_n))]
            zs[1, k] = f[part(f, pl.ds(k, cx_n, stride=cz_n))]
        copies = [
            send(cs.at[k], hold.at[k], *sem[k], to) for k, to in enumerate(corners)
        ]
        copies.append(send(zs.at[0], lo_z, *sem[4], north))
        copies.append(send(zs.at[1], hi_z, *sem[5], south))
        copies.append(send(f.at[part(f, pl.ds(last - cz_n, 2 * cz_n))], lo_x, *sem[6], east))
        copies.append(send(f.at[part(f, pl.ds(0, 2 * cz_n))], hi_x, *sem[7], west))
        return copies

    def arrive(copies):
        for copy in copies:
            copy.wait_recv()

    level = lax.broadcasted_iota(jnp.int32, (rows, ny), 1)
    depth = lax.rem(lax.broadcasted_iota(jnp.int32, (rows, ny), 0), cz_n)
    bottom = level == 0
    top = level == ny - 1
    front = depth == 0
    back = depth == cz_n - 1

    def spread(edge):
        wide = jnp.broadcast_to(edge[..., None, :], edge.shape[:-1] + (cz_n, ny))
        return wide.reshape(edge.shape[:-2] + (rows, ny))

    def x_prev(f, edge):
        return jnp.concatenate([edge, f[..., : rows - cz_n, :]], -2)

    def x_next(f, edge):
        return jnp.concatenate([f[..., cz_n:, :], edge], -2)

    def z_prev(f, edge):
        return jnp.where(front, spread(edge), pltpu.roll(f, 1, f.ndim - 2))

    def z_next(f, edge):
        return jnp.where(back, spread(edge), pltpu.roll(f, rows - 1, f.ndim - 2))

    def y_prev(f):
        return pltpu.roll(f, 1, f.ndim - 1)

    def y_next(f):
        return pltpu.roll(f, ny - 1, f.ndim - 1)

    halo0 = exchange(0, x0_ref, zsend, xlo, xhi, zlo, zhi)
    coef_send[...] = face_ref[1, pl.ds(cz_n - 1, cx_n, stride=cz_n), :]
    coefs = [
        send(face_ref.at[0, pl.ds(last, cz_n), :], coef_x, coef_ssem.at[0], coef_rsem.at[0], east),
        send(coef_send, coef_z, coef_ssem.at[1], coef_rsem.at[1], north),
    ]
    cy = face_ref[2]
    upper = jnp.where(top, 0.0, cy)
    lower = jnp.where(bottom, 0.0, y_prev(cy))
    wall = jnp.where(bottom | top, jnp.broadcast_to(cy[:, ny - 1 :], (rows, ny)), 0.0)
    coef[1] = face_ref[0]
    coef[3] = face_ref[1]
    coef[5] = upper
    coef[6] = lower
    loads[2].wait()
    base = diag_ref[...] + (face_ref[0] + face_ref[1]) + (upper + lower) + wall
    eye = lax.broadcasted_iota(jnp.int32, (cz_n, cz_n), 0) == lax.broadcasted_iota(
        jnp.int32, (cz_n, cz_n), 1
    )

    def column(side):
        flags = bc_ref[side].astype(jnp.float32)
        parts = [
            jnp.sum(
                jnp.where(eye, jnp.broadcast_to(flags[i : i + 1], (cz_n, cz_n)), 0.0),
                axis=1, keepdims=True,
            )
            for i in range(cx_n)
        ]
        return jnp.broadcast_to(jnp.concatenate(parts, 0), (rows, ny))

    arrive(coefs)
    west_c = x_prev(face_ref[0], coef_x[...])
    south_c = z_prev(face_ref[1], coef_z[...])
    coef[2] = west_c
    coef[4] = south_c
    coef[0] = base + (west_c + south_c)

    def apply(f, edges):
        total = coef[0] * f
        total -= coef[1] * x_next(f, edges[1]) + coef[2] * x_prev(f, edges[0])
        total -= coef[3] * z_next(f, edges[3]) + coef[4] * z_prev(f, edges[2])
        total -= coef[5] * y_next(f) + coef[6] * y_prev(f)
        return total

    edge_rows = (cz_n, cz_n, cx_n, cx_n)
    around = ((0, 1), (2, 3), (0, 2), (1, 3))

    def insides(ref):
        return (
            ref[part(ref, pl.ds(0, cz_n))],
            ref[part(ref, pl.ds(last, cz_n))],
            ref[part(ref, pl.ds(0, cx_n, stride=cz_n))],
            ref[part(ref, pl.ds(cz_n - 1, cx_n, stride=cz_n))],
        )

    def split(lo_x, hi_x, lo_z, hi_z):
        near = (lo_x[..., cz_n:, :], hi_x[..., :cz_n, :], lo_z[1], hi_z[0])
        far = (lo_x[..., :cz_n, :], hi_x[..., cz_n:, :], lo_z[0], hi_z[1])
        return near, far

    def along_face(k, f, before, after):
        n = edge_rows[k]
        pos = lax.broadcasted_iota(jnp.int32, (n, ny), 0)
        return (
            jnp.where(pos == 0, before, pltpu.roll(f, 1, f.ndim - 2)),
            jnp.where(pos == n - 1, after, pltpu.roll(f, n - 1, f.ndim - 2)),
        )

    face_coefs = (kxlo, kxhi, kzlo, kzhi)

    def apply_faces(ref, near, far, corner):
        out = []
        for k, inside in enumerate(insides(ref)):
            f, c = near[k], face_coefs[k]
            down, up = (far[k], inside) if k % 2 == 0 else (inside, far[k])
            before, after = along_face(k, f, corner[around[k][0]], corner[around[k][1]])
            n, t = (1, 3) if k < 2 else (3, 1)
            total = c[0] * f
            total -= c[n] * up + c[n + 1] * down
            total -= c[t] * after + c[t + 1] * before
            total -= c[5] * y_next(f) + c[6] * y_prev(f)
            out.append(total)
        return out

    def wide_field(i, ref):
        return exchange_wide(
            18 + 8 * i, ref, wzsend.at[i], wc_send.at[i],
            wxlo.at[i], wxhi.at[i], wzlo.at[i], wzhi.at[i], wc.at[i],
        )

    def wide_edges(i):
        near, far = split(wxlo[i], wxhi[i], wzlo[i], wzhi[i])
        return near, far, [wc[i, k] for k in range(4)]

    def dots(pairs):
        sums = [jnp.sum(a * b, axis=1, keepdims=True) for a, b in pairs]
        while len(sums) < PAD:
            sums.append(jnp.zeros_like(sums[0]))
        stack = jnp.concatenate(sums, 1).reshape(3 * PAD, ny)
        total = jnp.sum(stack, axis=1, keepdims=True)
        shape = (3 * PAD, 128)
        pick = lax.broadcasted_iota(jnp.int32, shape, 0) == lax.broadcasted_iota(
            jnp.int32, shape, 1
        )
        return jnp.sum(
            jnp.where(pick, jnp.broadcast_to(total, shape), 0.0), axis=0, keepdims=True
        )

    def scatter(msg, got, ssem, rsem, others):
        return [
            send(msg, got.at[d], ssem.at[d], rsem, to) for d, to in enumerate(others)
        ]

    def gathered(msg, got, rsem):
        pltpu.make_async_copy(got, got, rsem).wait()
        return msg[...] + jnp.sum(got[...], axis=0)

    def unpack(total):
        shape = (3 * PAD, 128)
        pick = lax.broadcasted_iota(jnp.int32, shape, 0) == lax.broadcasted_iota(
            jnp.int32, shape, 1
        )
        col = jnp.sum(
            jnp.where(pick, jnp.broadcast_to(total, shape), 0.0), axis=1, keepdims=True
        )
        wide = jnp.broadcast_to(col, (3 * PAD, ny)).reshape(3, PAD, ny)
        return [wide[:, k : k + 1] for k in range(PAD)]

    def sums_start(i, pairs):
        msg_x[i] = dots(pairs)
        scatter(msg_x.at[i], got_x.at[i], sum_sx.at[i], sum_rx.at[i], row_x)

    def sums_turn(i):
        msg_z[i] = gathered(msg_x.at[i], got_x.at[i], sum_rx.at[i])
        scatter(msg_z.at[i], got_z.at[i], sum_sz.at[i], sum_rz.at[i], row_z)

    def sums_end(i):
        return unpack(gathered(msg_z.at[i], got_z.at[i], sum_rz.at[i]))

    for load in loads[3:]:
        load.wait()
    arrive(halo0)
    fld[1] = src_ref[...] - apply(x0_ref[...], (xlo[...], xhi[...], zlo[...], zhi[...]))
    wide = wide_field(0, fld.at[1])
    aside = exchange(1, coef, kzsend, kxlo, kxhi, kzlo, kzhi)
    pdiag = 6.0 - jnp.where(bottom | top, 1.0, 0.0)
    pdiag = pdiag + jnp.where(bottom, column(0), 0.0) + jnp.where(top, column(1), 0.0)
    share = jacobi_weight / pdiag
    prs[4, 0] = pdiag
    arrive(wide)
    r_near, r_far, r_corner = wide_edges(0)
    v = apply(fld[1], r_near)
    fld[2] = v
    arrive(aside)
    v_near = apply_faces(fld.at[1], r_near, r_far, r_corner)
    fld[3] = apply(v, v_near)
    wide = wide_field(1, fld.at[3])
    r, v, u = fld[1], fld[2], fld[3]
    sums_start(0, [(r, r), (r, v), (r, u), (v, v), (v, u), (u, u)])
    aside = exchange_wide(
        0, map_ref, mzsend, mc_send, mxlo, mxhi, mzlo, mzhi, mc
    )
    aside.append(send(inv_ref, inv_w, side_s.at[16], side_r.at[16], east))
    aside.append(send(inv_ref, inv_e, side_s.at[17], side_r.at[17], west))
    aside += exchange(
        8, prs.at[4], dzsend, dxlo, dxhi, dzlo, dzhi
    )
    sums_turn(0)
    arrive(wide)
    u_near, u_far, u_corner = wide_edges(1)
    y = apply(fld[3], u_near)
    fld[4] = y
    y_near = apply_faces(fld.at[3], u_near, u_far, u_corner)
    z = apply(y, y_near)
    rr, rv, ru, vv, vu, uu = sums_end(0)[:6]
    alpha = rr / rv
    omega = (rv - alpha * (vv + ru) + alpha * alpha * vu) / (
        vv - 2.0 * alpha * vu + alpha * alpha * uu
    )
    rho_new = (rr - alpha * rv) - omega * (rv - alpha * ru)
    beta = (rho_new / rr) * (alpha / omega)

    def first(x, r, v, u, y, a, w, b):
        s = r - a * v
        t = v - a * u
        x1 = x + a * r + w * s
        r1 = s - w * t
        p2 = r1 + b * (r - w * v)
        mr1 = t - w * (u - a * y)
        v2 = mr1 + b * (v - w * u)
        return x1, r1, p2, v2, mr1

    r, v, u, y = fld[1], fld[2], fld[3], fld[4]
    x1, r1, p2, v2, mr1 = first(x0_ref[...], r, v, u, y, alpha, omega, beta)
    mv2 = (u - alpha * y) - omega * (y - alpha * z) + beta * (u - omega * y)
    sums_start(
        1,
        [(r, v2), (r1, mr1), (r1, mv2), (v2, mr1), (v2, mv2), (mr1, mr1), (mr1, mv2), (mv2, mv2)],
    )
    fld[5] = x1
    fld[6] = r1
    fld[7] = p2
    fld[8] = v2

    def edge_of(k, c):
        start = (xlo, xhi, zlo, zhi)[k]
        return first(
            start[c], r_near[k][c], v_near[k][c], u_near[k][c], y_near[k][c],
            alpha[c], omega[c], beta[c],
        )[:4]

    edge_x = edge_of(0, 0)
    edge_z = edge_of(2, 1)
    sums_turn(1)
    rv2, k1, k2, k3, k4, k5, k6, k7 = sums_end(1)
    alpha2 = rho_new / rv2
    omega2 = (k1 - alpha2 * (k2 + k3) + alpha2 * alpha2 * k4) / (
        k5 - 2.0 * alpha2 * k6 + alpha2 * alpha2 * k7
    )

    def second(x1, r1, p2, v2, a, w):
        return x1 + a * p2, w * (r1 - a * v2)

    def put(i, src, dst):
        copy = pltpu.make_async_copy(src, dst, store_sem.at[i])
        copy.start()
        return copy

    first_half, second_half = second(fld[5], fld[6], fld[7], fld[8], alpha2, omega2)
    fld[0] = first_half
    fld[9] = second_half
    stores = [put(0, fld.at[0], vel_a), put(1, fld.at[9], vel_b)]
    velocity = first_half + second_half
    west_u = sum(second(*edge_x, alpha2[0], omega2[0]))
    south_w = sum(second(*edge_z, alpha2[1], omega2[1]))
    ux, uz, uy = velocity[0], velocity[1], velocity[2]
    div = (ux - x_prev(ux, west_u)) + (uz - z_prev(uz, south_w))
    div = div + (uy - jnp.where(bottom, 0.0, y_prev(uy)))

    def operate(f, edges):
        near = x_next(f, edges[1]) + x_prev(f, edges[0])
        near += z_next(f, edges[3]) + z_prev(f, edges[2])
        near += jnp.where(top, 0.0, y_next(f)) + jnp.where(bottom, 0.0, y_prev(f))
        return pdiag * f - near

    def at_face(k, f, beyond, inside, before, after):
        lane = lax.broadcasted_iota(jnp.int32, f.shape, 1)
        before, after = along_face(k, f, before, after)
        near = (beyond + inside) + (before + after)
        near += jnp.where(lane == ny - 1, 0.0, y_next(f)) + jnp.where(lane == 0, 0.0, y_prev(f))
        return face_d[k] * f - near

    def operate_faces(ref, near, far, corner):
        return [
            at_face(k, near[k], far[k], inside, corner[around[k][0]], corner[around[k][1]])
            for k, inside in enumerate(insides(ref))
        ]

    q = share * div
    qref = prs.at[0, 0]
    qref[...] = q
    wide = exchange_wide(8, qref, qzsend, qc_send, qxlo, qxhi, qzlo, qzhi, qc)
    arrive(aside)
    face_d = (dxlo[0], dxhi[0], dzlo[0], dzhi[0])
    face_share = [jacobi_weight / d for d in face_d]
    arrive(wide)
    near, far = split(qxlo[...], qxhi[...], qzlo[...], qzhi[...])
    edges = [
        2.0 * near[k] - face_share[k] * out
        for k, out in enumerate(operate_faces(qref, near, far, [qc[k] for k in range(4)]))
    ]
    q = 2.0 * q - share * operate(q, near)
    res = div - operate(q, edges)
    cells = map_ref[...]
    parts = [
        jnp.sum(jnp.where(cells == m, res, 0.0), axis=0, keepdims=True) for m in range(COARSE)
    ]
    total = jnp.sum(jnp.concatenate(parts, 0), axis=1, keepdims=True)
    shape = (COARSE, lanes)
    place = lax.broadcasted_iota(jnp.int32, shape, 1) == (
        lax.broadcasted_iota(jnp.int32, shape, 0) + gz * COARSE
    )
    msg_c[...] = jnp.sum(
        jnp.where(place, jnp.broadcast_to(total, shape), 0.0), axis=0, keepdims=True
    )
    side = n_gz - 1
    scatter(msg_c, got_w, coarse_s.at[pl.ds(0, n_gz)], coarse_r.at[0], [east] + aside_e)
    scatter(msg_c, got_e, coarse_s.at[pl.ds(n_gz, n_gz)], coarse_r.at[1], [west] + aside_w)
    scatter(msg_c, got_c, coarse_s.at[pl.ds(2 * n_gz, side)], coarse_r.at[2], row_z)
    q = q + share * res
    prs[1, 0] = q
    halo = exchange_pressure(1)
    arrive(halo)
    q = q + share * (div - operate(q, (pxlo[1, 0], pxhi[1, 0], pzlo[1, 0], pzhi[1, 0])))
    prs[3, 0] = q
    stores.append(put(2, prs.at[3, 0], prs_a))

    spots = (south[1], gz, north[1])

    def corrections(inv, coarse):
        out = []
        for spot in spots:
            block = inv[pl.ds(pl.multiple_of(spot * COARSE, COARSE), COARSE), :]
            col = jnp.sum(block * coarse[:, : block.shape[1]], axis=1, keepdims=True)
            out.append(jnp.broadcast_to(col, (COARSE, ny)))
        return out

    def lift(cell, corr):
        add = jnp.broadcast_to(corr[0:1], cell.shape)
        for m in range(1, COARSE):
            add = jnp.where(cell == m, corr[m : m + 1], add)
        return add

    def whole(got, rsem):
        pltpu.make_async_copy(got, got, rsem).wait()
        return jnp.sum(got[...], axis=0)

    south_k, own_k, north_k = corrections(inv_ref, gathered(msg_c, got_c, coarse_r.at[2]))
    west_k = corrections(inv_w, whole(got_w, coarse_r.at[0]))
    east_k = corrections(inv_e, whole(got_e, coarse_r.at[1]))
    e = lift(cells, own_k)
    eref = prs.at[2, 0]
    eref[...] = e
    near, far = split(
        lift(mxlo[...], west_k[1]),
        lift(mxhi[...], east_k[1]),
        lift(mzlo[...], south_k),
        lift(mzhi[...], north_k),
    )
    points = [
        lift(mc[k], c) for k, c in enumerate((west_k[0], west_k[2], east_k[0], east_k[2]))
    ]
    edges = [
        near[k] - face_share[k] * out
        for k, out in enumerate(operate_faces(eref, near, far, points))
    ]
    e = e - share * operate(e, near)
    e = e - share * operate(e, edges)
    prs[5, 0] = e
    stores.append(put(3, prs.at[5, 0], prs_b))
    for copy in stores:
        copy.wait()
    for copy in pending:
        copy.wait_send()


def body(n_gx, n_gz, velocity_old, source, diag_coef, face_coef, bc_flags, coarse_map, coarse_inverse):
    cx_n, cz_n, ny = diag_coef.shape
    rows = cx_n * cz_n
    group = coarse_inverse.shape[1]
    lanes = -(-group // 128) * 128
    f32 = jnp.float32
    vmem = pltpu.VMEM
    dma = pltpu.SemaphoreType.DMA

    def wide_set(kind):
        return [
            vmem((2 * cz_n, ny), kind),
            vmem((2 * cz_n, ny), kind),
            vmem((2, cx_n, ny), kind),
            vmem((2, cx_n, ny), kind),
            vmem((2, 2, cx_n, ny), kind),
            vmem((4, 1, ny), kind),
            vmem((4, 1, ny), kind),
        ]

    scratch = [
        vmem((3, rows, ny), f32),
        vmem((3, rows, ny), f32),
        vmem((rows, ny), f32),
        vmem((3, rows, ny), f32),
        vmem(bc_flags.shape, jnp.int32),
        vmem((rows, ny), jnp.int32),
        vmem(coarse_inverse.shape, f32),
        vmem((10, 3, rows, ny), f32),
        vmem((3, cz_n, ny), f32),
        vmem((3, cz_n, ny), f32),
        vmem((3, cx_n, ny), f32),
        vmem((3, cx_n, ny), f32),
        vmem((2, 3, cx_n, ny), f32),
        vmem((2, 3, 2 * cz_n, ny), f32),
        vmem((2, 3, 2 * cz_n, ny), f32),
        vmem((2, 2, 3, cx_n, ny), f32),
        vmem((2, 2, 3, cx_n, ny), f32),
        vmem((2, 2, 2, 3, cx_n, ny), f32),
        vmem((2, 4, 3, 1, ny), f32),
        vmem((2, 4, 3, 1, ny), f32),
        vmem((cx_n, ny), f32),
        vmem((cz_n, ny), f32),
        vmem((cx_n, ny), f32),
        vmem((6, 1, rows, ny), f32),
        vmem((2, 1, cz_n, ny), f32),
        vmem((2, 1, cz_n, ny), f32),
        vmem((2, 1, cx_n, ny), f32),
        vmem((2, 1, cx_n, ny), f32),
        vmem((2, 2, 1, cx_n, ny), f32),
        *wide_set(f32),
        *wide_set(jnp.int32),
        vmem((1, cz_n, ny), f32),
        vmem((1, cz_n, ny), f32),
        vmem((1, cx_n, ny), f32),
        vmem((1, cx_n, ny), f32),
        vmem((2, 1, cx_n, ny), f32),
        vmem(coarse_inverse.shape, f32),
        vmem(coarse_inverse.shape, f32),
        vmem((7, rows, ny), f32),
        vmem((7, cz_n, ny), f32),
        vmem((7, cz_n, ny), f32),
        vmem((7, cx_n, ny), f32),
        vmem((7, cx_n, ny), f32),
        vmem((2, 7, cx_n, ny), f32),
        vmem((2, 1, 128), f32),
        vmem((2, n_gx - 1, 1, 128), f32),
        vmem((2, 1, 128), f32),
        vmem((2, n_gz - 1, 1, 128), f32),
        vmem((1, lanes), f32),
        vmem((n_gz - 1, 1, lanes), f32),
        vmem((n_gz, 1, lanes), f32),
        vmem((n_gz, 1, lanes), f32),
        dma((9, 4)),
        dma((9, 4)),
        dma((2,)),
        dma((2,)),
        dma((2, n_gx - 1)),
        dma((2,)),
        dma((2, n_gz - 1)),
        dma((2,)),
        dma((3 * n_gz - 1,)),
        dma((3,)),
        dma((7,)),
        dma((34,)),
        dma((34,)),
        dma((4,)),
    ]
    spec = pl.BlockSpec(memory_space=pltpu.HBM)
    vel_a, vel_b, prs_a, prs_b = pl.pallas_call(
        functools.partial(kernel, (n_gx, n_gz, cx_n, cz_n, ny, lanes)),
        out_shape=(
            jax.ShapeDtypeStruct((3, rows, ny), f32),
            jax.ShapeDtypeStruct((3, rows, ny), f32),
            jax.ShapeDtypeStruct((rows, ny), f32),
            jax.ShapeDtypeStruct((rows, ny), f32),
        ),
        in_specs=[spec] * 7,
        out_specs=(spec,) * 4,
        scratch_shapes=scratch,
        compiler_params=pltpu.CompilerParams(
            collective_id=0, has_side_effects=True
        ),
        name="corrector",
    )(
        velocity_old.reshape(3, rows, ny),
        source.reshape(3, rows, ny),
        diag_coef.reshape(rows, ny),
        face_coef.reshape(3, rows, ny),
        bc_flags,
        coarse_map.reshape(rows, ny),
        coarse_inverse,
    )
    velocity = (vel_a + vel_b).reshape(3, cx_n, cz_n, ny)
    return velocity, (prs_a + prs_b).reshape(cx_n, cz_n, ny)


def solution(mesh):
    placed = (
        P(None, "gx", "gz", None),
        P(None, "gx", "gz", None),
        P("gx", "gz", None),
        P(None, "gx", "gz", None),
        P(None, "gx", "gz"),
        P("gx", "gz", None),
        P("gx", None),
    )
    return jax.shard_map(
        functools.partial(body, mesh.shape["gx"], mesh.shape["gz"]),
        mesh=mesh,
        in_specs=placed,
        out_specs=(P(None, "gx", "gz", None), P("gx", "gz", None)),
        check_vma=False,
    )
```

```python
import functools

import jax
import jax.numpy as jnp
from jax import lax
from jax.experimental import pallas as pl
from jax.experimental.pallas import tpu as pltpu
from jax.sharding import PartitionSpec as P

COARSE = 16
PAD = 8

jacobi_weight = 2.0 / 3.0
MESH = pl.DeviceIdType.MESH


def kernel(
    dims,
    x0_in, src_in, diag_in, face_in, bc_in, map_in, inv_in,
    vel_ref, out_ref,
    x0_ref, src_ref, diag_ref, face_ref, bc_ref, map_ref, inv_ref,
    fld, xlo, xhi, zlo, zhi, zsend,
    wxlo, wxhi, wzlo, wzhi, wzsend, wc_send, wc,
    coef_send, coef_x, coef_z,
    prs, pxlo, pxhi, pzlo, pzhi, pzsend,
    qxlo, qxhi, qzlo, qzhi, qzsend, qc_send, qc,
    mxlo, mxhi, mzlo, mzhi, mzsend, mc_send, mc,
    dxlo, dxhi, dzlo, dzhi, dzsend, inv_w, inv_e,
    coef, kxlo, kxhi, kzlo, kzhi, kzsend,
    msg_x, got_x, msg_z, got_z, msg_c, got_c, got_w, got_e,
    send_sem, recv_sem, coef_ssem, coef_rsem,
    sum_sx, sum_rx, sum_sz, sum_rz, coarse_s, coarse_r,
    load_sem, side_s, side_r,
):
    n_gx, n_gz, cx_n, cz_n, ny, lanes = dims
    rows = cx_n * cz_n
    gx = lax.axis_index("gx")
    gz = lax.axis_index("gz")
    east = (lax.rem(gx + 1, n_gx), gz)
    west = (lax.rem(gx + n_gx - 1, n_gx), gz)
    north = (gx, lax.rem(gz + 1, n_gz))
    south = (gx, lax.rem(gz + n_gz - 1, n_gz))
    row_x = [(lax.rem(gx + d, n_gx), gz) for d in range(1, n_gx)]
    row_z = [(gx, lax.rem(gz + d, n_gz)) for d in range(1, n_gz)]
    pending = []

    def send(src, dst, ssem, rsem, to):
        copy = pltpu.make_async_remote_copy(
            src_ref=src, dst_ref=dst, send_sem=ssem, recv_sem=rsem,
            device_id=to, device_id_type=MESH,
        )
        copy.start()
        pending.append(copy)
        return copy

    aside_w = [(west[0], to[1]) for to in row_z]
    aside_e = [(east[0], to[1]) for to in row_z]
    corners = [
        (east[0], north[1]), (east[0], south[1]), (west[0], north[1]), (west[0], south[1])
    ]
    loads = [
        pltpu.make_async_copy(a, b, load_sem.at[i])
        for i, (a, b) in enumerate(
            [
                (x0_in, x0_ref), (face_in, face_ref), (diag_in, diag_ref), (src_in, src_ref),
                (bc_in, bc_ref), (map_in, map_ref), (inv_in, inv_ref),
            ]
        )
    ]
    for load in loads:
        load.start()
    barrier = pltpu.get_barrier_semaphore()
    partners = row_x + row_z + aside_w + aside_e
    for other in partners:
        pl.semaphore_signal(barrier, inc=1, device_id=other, device_id_type=MESH)
    loads[0].wait()
    loads[1].wait()
    pl.semaphore_wait(barrier, len(partners))

    last = rows - cz_n

    def exchange(phase, src, zs, lo_x, hi_x, lo_z, hi_z):
        zs[0] = src[:, pl.ds(cz_n - 1, cx_n, stride=cz_n), :]
        zs[1] = src[:, pl.ds(0, cx_n, stride=cz_n), :]
        sems = [(send_sem.at[phase, i], recv_sem.at[phase, i]) for i in range(4)]
        return [
            send(zs.at[0], lo_z, *sems[2], north),
            send(zs.at[1], hi_z, *sems[3], south),
            send(src.at[:, pl.ds(last, cz_n), :], lo_x, *sems[0], east),
            send(src.at[:, pl.ds(0, cz_n), :], hi_x, *sems[1], west),
        ]

    def exchange_pressure(i):
        return exchange(
            5 + i, prs.at[i], pzsend.at[i], pxlo.at[i], pxhi.at[i], pzlo.at[i], pzhi.at[i]
        )

    def part(ref, which):
        return (slice(None),) * (len(ref.shape) - 2) + (which, slice(None))

    def exchange_wide(base, f, zs, cs, lo_x, hi_x, lo_z, hi_z, hold):
        sem = [(side_s.at[base + i], side_r.at[base + i]) for i in range(8)]
        for k, r in enumerate((rows - 1, last, cz_n - 1, 0)):
            cs[k] = f[part(f, pl.ds(r, 1))]
        for k in range(2):
            zs[0, k] = f[part(f, pl.ds(cz_n - 2 + k, cx_n, stride=cz_n))]
            zs[1, k] = f[part(f, pl.ds(k, cx_n, stride=cz_n))]
        copies = [
            send(cs.at[k], hold.at[k], *sem[k], to) for k, to in enumerate(corners)
        ]
        copies.append(send(zs.at[0], lo_z, *sem[4], north))
        copies.append(send(zs.at[1], hi_z, *sem[5], south))
        copies.append(send(f.at[part(f, pl.ds(last - cz_n, 2 * cz_n))], lo_x, *sem[6], east))
        copies.append(send(f.at[part(f, pl.ds(0, 2 * cz_n))], hi_x, *sem[7], west))
        return copies

    def arrive(copies):
        for copy in copies:
            copy.wait_recv()

    level = lax.broadcasted_iota(jnp.int32, (rows, ny), 1)
    depth = lax.rem(lax.broadcasted_iota(jnp.int32, (rows, ny), 0), cz_n)
    bottom = level == 0
    top = level == ny - 1
    front = depth == 0
    back = depth == cz_n - 1

    def spread(edge):
        wide = jnp.broadcast_to(edge[..., None, :], edge.shape[:-1] + (cz_n, ny))
        return wide.reshape(edge.shape[:-2] + (rows, ny))

    def x_prev(f, edge):
        return jnp.concatenate([edge, f[..., : rows - cz_n, :]], -2)

    def x_next(f, edge):
        return jnp.concatenate([f[..., cz_n:, :], edge], -2)

    def z_prev(f, edge):
        return jnp.where(front, spread(edge), pltpu.roll(f, 1, f.ndim - 2))

    def z_next(f, edge):
        return jnp.where(back, spread(edge), pltpu.roll(f, rows - 1, f.ndim - 2))

    def y_prev(f):
        return pltpu.roll(f, 1, f.ndim - 1)

    def y_next(f):
        return pltpu.roll(f, ny - 1, f.ndim - 1)

    halo0 = exchange(0, x0_ref, zsend, xlo, xhi, zlo, zhi)
    coef_send[...] = face_ref[1, pl.ds(cz_n - 1, cx_n, stride=cz_n), :]
    coefs = [
        send(face_ref.at[0, pl.ds(last, cz_n), :], coef_x, coef_ssem.at[0], coef_rsem.at[0], east),
        send(coef_send, coef_z, coef_ssem.at[1], coef_rsem.at[1], north),
    ]
    cy = face_ref[2]
    upper = jnp.where(top, 0.0, cy)
    lower = jnp.where(bottom, 0.0, y_prev(cy))
    wall = jnp.where(bottom | top, jnp.broadcast_to(cy[:, ny - 1 :], (rows, ny)), 0.0)
    coef[1] = face_ref[0]
    coef[3] = face_ref[1]
    coef[5] = upper
    coef[6] = lower
    loads[2].wait()
    base = diag_ref[...] + (face_ref[0] + face_ref[1]) + (upper + lower) + wall
    eye = lax.broadcasted_iota(jnp.int32, (cz_n, cz_n), 0) == lax.broadcasted_iota(
        jnp.int32, (cz_n, cz_n), 1
    )

    def column(side):
        flags = bc_ref[side].astype(jnp.float32)
        parts = [
            jnp.sum(
                jnp.where(eye, jnp.broadcast_to(flags[i : i + 1], (cz_n, cz_n)), 0.0),
                axis=1, keepdims=True,
            )
            for i in range(cx_n)
        ]
        return jnp.broadcast_to(jnp.concatenate(parts, 0), (rows, ny))

    arrive(coefs)
    west_c = x_prev(face_ref[0], coef_x[...])
    south_c = z_prev(face_ref[1], coef_z[...])
    coef[2] = west_c
    coef[4] = south_c
    coef[0] = base + (west_c + south_c)

    def apply(f, edges):
        total = coef[0] * f
        total -= coef[1] * x_next(f, edges[1]) + coef[2] * x_prev(f, edges[0])
        total -= coef[3] * z_next(f, edges[3]) + coef[4] * z_prev(f, edges[2])
        total -= coef[5] * y_next(f) + coef[6] * y_prev(f)
        return total

    edge_rows = (cz_n, cz_n, cx_n, cx_n)
    around = ((0, 1), (2, 3), (0, 2), (1, 3))

    def insides(ref):
        return (
            ref[part(ref, pl.ds(0, cz_n))],
            ref[part(ref, pl.ds(last, cz_n))],
            ref[part(ref, pl.ds(0, cx_n, stride=cz_n))],
            ref[part(ref, pl.ds(cz_n - 1, cx_n, stride=cz_n))],
        )

    def split(lo_x, hi_x, lo_z, hi_z):
        near = (lo_x[..., cz_n:, :], hi_x[..., :cz_n, :], lo_z[1], hi_z[0])
        far = (lo_x[..., :cz_n, :], hi_x[..., cz_n:, :], lo_z[0], hi_z[1])
        return near, far

    def along_face(k, f, before, after):
        n = edge_rows[k]
        pos = lax.broadcasted_iota(jnp.int32, (n, ny), 0)
        return (
            jnp.where(pos == 0, before, pltpu.roll(f, 1, f.ndim - 2)),
            jnp.where(pos == n - 1, after, pltpu.roll(f, n - 1, f.ndim - 2)),
        )

    face_coefs = (kxlo, kxhi, kzlo, kzhi)

    def apply_faces(ref, near, far, corner):
        out = []
        for k, inside in enumerate(insides(ref)):
            f, c = near[k], face_coefs[k]
            down, up = (far[k], inside) if k % 2 == 0 else (inside, far[k])
            before, after = along_face(k, f, corner[around[k][0]], corner[around[k][1]])
            n, t = (1, 3) if k < 2 else (3, 1)
            total = c[0] * f
            total -= c[n] * up + c[n + 1] * down
            total -= c[t] * after + c[t + 1] * before
            total -= c[5] * y_next(f) + c[6] * y_prev(f)
            out.append(total)
        return out

    def wide_field(i, ref):
        return exchange_wide(
            18 + 8 * i, ref, wzsend.at[i], wc_send.at[i],
            wxlo.at[i], wxhi.at[i], wzlo.at[i], wzhi.at[i], wc.at[i],
        )

    def wide_edges(i):
        near, far = split(wxlo[i], wxhi[i], wzlo[i], wzhi[i])
        return near, far, [wc[i, k] for k in range(4)]

    def dots(pairs):
        sums = [jnp.sum(a * b, axis=1, keepdims=True) for a, b in pairs]
        while len(sums) < PAD:
            sums.append(jnp.zeros_like(sums[0]))
        stack = jnp.concatenate(sums, 1).reshape(3 * PAD, ny)
        total = jnp.sum(stack, axis=1, keepdims=True)
        shape = (3 * PAD, 128)
        pick = lax.broadcasted_iota(jnp.int32, shape, 0) == lax.broadcasted_iota(
            jnp.int32, shape, 1
        )
        return jnp.sum(
            jnp.where(pick, jnp.broadcast_to(total, shape), 0.0), axis=0, keepdims=True
        )

    def scatter(msg, got, ssem, rsem, others):
        return [
            send(msg, got.at[d], ssem.at[d], rsem, to) for d, to in enumerate(others)
        ]

    def gathered(msg, got, rsem):
        pltpu.make_async_copy(got, got, rsem).wait()
        return msg[...] + jnp.sum(got[...], axis=0)

    def unpack(total):
        shape = (3 * PAD, 128)
        pick = lax.broadcasted_iota(jnp.int32, shape, 0) == lax.broadcasted_iota(
            jnp.int32, shape, 1
        )
        col = jnp.sum(
            jnp.where(pick, jnp.broadcast_to(total, shape), 0.0), axis=1, keepdims=True
        )
        wide = jnp.broadcast_to(col, (3 * PAD, ny)).reshape(3, PAD, ny)
        return [wide[:, k : k + 1] for k in range(PAD)]

    def sums_start(i, pairs):
        msg_x[i] = dots(pairs)
        scatter(msg_x.at[i], got_x.at[i], sum_sx.at[i], sum_rx.at[i], row_x)

    def sums_turn(i):
        msg_z[i] = gathered(msg_x.at[i], got_x.at[i], sum_rx.at[i])
        scatter(msg_z.at[i], got_z.at[i], sum_sz.at[i], sum_rz.at[i], row_z)

    def sums_end(i):
        return unpack(gathered(msg_z.at[i], got_z.at[i], sum_rz.at[i]))

    for load in loads[3:]:
        load.wait()
    arrive(halo0)
    fld[1] = src_ref[...] - apply(x0_ref[...], (xlo[...], xhi[...], zlo[...], zhi[...]))
    wide = wide_field(0, fld.at[1])
    aside = exchange(1, coef, kzsend, kxlo, kxhi, kzlo, kzhi)
    pdiag = 6.0 - jnp.where(bottom | top, 1.0, 0.0)
    pdiag = pdiag + jnp.where(bottom, column(0), 0.0) + jnp.where(top, column(1), 0.0)
    share = jacobi_weight / pdiag
    prs[4, 0] = pdiag
    arrive(wide)
    r_near, r_far, r_corner = wide_edges(0)
    v = apply(fld[1], r_near)
    fld[2] = v
    arrive(aside)
    v_near = apply_faces(fld.at[1], r_near, r_far, r_corner)
    fld[3] = apply(v, v_near)
    wide = wide_field(1, fld.at[3])
    r, v, u = fld[1], fld[2], fld[3]
    sums_start(0, [(r, r), (r, v), (r, u), (v, v), (v, u), (u, u)])
    aside = exchange_wide(
        0, map_ref, mzsend, mc_send, mxlo, mxhi, mzlo, mzhi, mc
    )
    aside.append(send(inv_ref, inv_w, side_s.at[16], side_r.at[16], east))
    aside.append(send(inv_ref, inv_e, side_s.at[17], side_r.at[17], west))
    aside += exchange(
        8, prs.at[4], dzsend, dxlo, dxhi, dzlo, dzhi
    )
    sums_turn(0)
    arrive(wide)
    u_near, u_far, u_corner = wide_edges(1)
    y = apply(fld[3], u_near)
    fld[4] = y
    y_near = apply_faces(fld.at[3], u_near, u_far, u_corner)
    z = apply(y, y_near)
    rr, rv, ru, vv, vu, uu = sums_end(0)[:6]
    alpha = rr / rv
    omega = (rv - alpha * (vv + ru) + alpha * alpha * vu) / (
        vv - 2.0 * alpha * vu + alpha * alpha * uu
    )
    rho_new = (rr - alpha * rv) - omega * (rv - alpha * ru)
    beta = (rho_new / rr) * (alpha / omega)

    def first(x, r, v, u, y, a, w, b):
        s = r - a * v
        t = v - a * u
        x1 = x + a * r + w * s
        r1 = s - w * t
        p2 = r1 + b * (r - w * v)
        mr1 = t - w * (u - a * y)
        v2 = mr1 + b * (v - w * u)
        return x1, r1, p2, v2, mr1

    r, v, u, y = fld[1], fld[2], fld[3], fld[4]
    x1, r1, p2, v2, mr1 = first(x0_ref[...], r, v, u, y, alpha, omega, beta)
    mv2 = (u - alpha * y) - omega * (y - alpha * z) + beta * (u - omega * y)
    sums_start(
        1,
        [(r, v2), (r1, mr1), (r1, mv2), (v2, mr1), (v2, mv2), (mr1, mr1), (mr1, mv2), (mv2, mv2)],
    )
    fld[5] = x1
    fld[6] = r1
    fld[7] = p2
    fld[8] = v2

    def edge_of(k, c):
        start = (xlo, xhi, zlo, zhi)[k]
        return first(
            start[c], r_near[k][c], v_near[k][c], u_near[k][c], y_near[k][c],
            alpha[c], omega[c], beta[c],
        )[:4]

    edge_x = edge_of(0, 0)
    edge_z = edge_of(2, 1)
    sums_turn(1)
    rv2, k1, k2, k3, k4, k5, k6, k7 = sums_end(1)
    alpha2 = rho_new / rv2
    omega2 = (k1 - alpha2 * (k2 + k3) + alpha2 * alpha2 * k4) / (
        k5 - 2.0 * alpha2 * k6 + alpha2 * alpha2 * k7
    )

    def second(x1, r1, p2, v2, a, w):
        return x1 + a * p2 + w * (r1 - a * v2)

    velocity = second(fld[5], fld[6], fld[7], fld[8], alpha2, omega2)
    vel_ref[...] = velocity
    west_u = second(*edge_x, alpha2[0], omega2[0])
    south_w = second(*edge_z, alpha2[1], omega2[1])
    ux, uz, uy = velocity[0], velocity[1], velocity[2]
    div = (ux - x_prev(ux, west_u)) + (uz - z_prev(uz, south_w))
    div = div + (uy - jnp.where(bottom, 0.0, y_prev(uy)))

    def operate(f, edges):
        near = x_next(f, edges[1]) + x_prev(f, edges[0])
        near += z_next(f, edges[3]) + z_prev(f, edges[2])
        near += jnp.where(top, 0.0, y_next(f)) + jnp.where(bottom, 0.0, y_prev(f))
        return pdiag * f - near

    def at_face(k, f, beyond, inside, before, after):
        lane = lax.broadcasted_iota(jnp.int32, f.shape, 1)
        before, after = along_face(k, f, before, after)
        near = (beyond + inside) + (before + after)
        near += jnp.where(lane == ny - 1, 0.0, y_next(f)) + jnp.where(lane == 0, 0.0, y_prev(f))
        return face_d[k] * f - near

    def operate_faces(ref, near, far, corner):
        return [
            at_face(k, near[k], far[k], inside, corner[around[k][0]], corner[around[k][1]])
            for k, inside in enumerate(insides(ref))
        ]

    q = share * div
    qref = prs.at[0, 0]
    qref[...] = q
    wide = exchange_wide(8, qref, qzsend, qc_send, qxlo, qxhi, qzlo, qzhi, qc)
    arrive(aside)
    face_d = (dxlo[0], dxhi[0], dzlo[0], dzhi[0])
    face_share = [jacobi_weight / d for d in face_d]
    arrive(wide)
    near, far = split(qxlo[...], qxhi[...], qzlo[...], qzhi[...])
    edges = [
        2.0 * near[k] - face_share[k] * out
        for k, out in enumerate(operate_faces(qref, near, far, [qc[k] for k in range(4)]))
    ]
    q = 2.0 * q - share * operate(q, near)
    res = div - operate(q, edges)
    cells = map_ref[...]
    parts = [
        jnp.sum(jnp.where(cells == m, res, 0.0), axis=0, keepdims=True) for m in range(COARSE)
    ]
    total = jnp.sum(jnp.concatenate(parts, 0), axis=1, keepdims=True)
    shape = (COARSE, lanes)
    place = lax.broadcasted_iota(jnp.int32, shape, 1) == (
        lax.broadcasted_iota(jnp.int32, shape, 0) + gz * COARSE
    )
    msg_c[...] = jnp.sum(
        jnp.where(place, jnp.broadcast_to(total, shape), 0.0), axis=0, keepdims=True
    )
    side = n_gz - 1
    scatter(msg_c, got_w, coarse_s.at[pl.ds(0, n_gz)], coarse_r.at[0], [east] + aside_e)
    scatter(msg_c, got_e, coarse_s.at[pl.ds(n_gz, n_gz)], coarse_r.at[1], [west] + aside_w)
    scatter(msg_c, got_c, coarse_s.at[pl.ds(2 * n_gz, side)], coarse_r.at[2], row_z)
    q = q + share * res
    prs[1, 0] = q
    halo = exchange_pressure(1)
    arrive(halo)
    q = q + share * (div - operate(q, (pxlo[1, 0], pxhi[1, 0], pzlo[1, 0], pzhi[1, 0])))

    spots = (south[1], gz, north[1])

    def corrections(inv, coarse):
        out = []
        for spot in spots:
            block = inv[pl.ds(pl.multiple_of(spot * COARSE, COARSE), COARSE), :]
            col = jnp.sum(block * coarse[:, : block.shape[1]], axis=1, keepdims=True)
            out.append(jnp.broadcast_to(col, (COARSE, ny)))
        return out

    def lift(cell, corr):
        add = jnp.broadcast_to(corr[0:1], cell.shape)
        for m in range(1, COARSE):
            add = jnp.where(cell == m, corr[m : m + 1], add)
        return add

    def whole(got, rsem):
        pltpu.make_async_copy(got, got, rsem).wait()
        return jnp.sum(got[...], axis=0)

    south_k, own_k, north_k = corrections(inv_ref, gathered(msg_c, got_c, coarse_r.at[2]))
    west_k = corrections(inv_w, whole(got_w, coarse_r.at[0]))
    east_k = corrections(inv_e, whole(got_e, coarse_r.at[1]))
    e = lift(cells, own_k)
    eref = prs.at[2, 0]
    eref[...] = e
    near, far = split(
        lift(mxlo[...], west_k[1]),
        lift(mxhi[...], east_k[1]),
        lift(mzlo[...], south_k),
        lift(mzhi[...], north_k),
    )
    points = [
        lift(mc[k], c) for k, c in enumerate((west_k[0], west_k[2], east_k[0], east_k[2]))
    ]
    edges = [
        near[k] - face_share[k] * out
        for k, out in enumerate(operate_faces(eref, near, far, points))
    ]
    e = e - share * operate(e, near)
    e = e - share * operate(e, edges)
    out_ref[...] = q + e
    for copy in pending:
        copy.wait_send()


def body(n_gx, n_gz, velocity_old, source, diag_coef, face_coef, bc_flags, coarse_map, coarse_inverse):
    cx_n, cz_n, ny = diag_coef.shape
    rows = cx_n * cz_n
    group = coarse_inverse.shape[1]
    lanes = -(-group // 128) * 128
    f32 = jnp.float32
    vmem = pltpu.VMEM
    dma = pltpu.SemaphoreType.DMA

    def wide_set(kind):
        return [
            vmem((2 * cz_n, ny), kind),
            vmem((2 * cz_n, ny), kind),
            vmem((2, cx_n, ny), kind),
            vmem((2, cx_n, ny), kind),
            vmem((2, 2, cx_n, ny), kind),
            vmem((4, 1, ny), kind),
            vmem((4, 1, ny), kind),
        ]

    scratch = [
        vmem((3, rows, ny), f32),
        vmem((3, rows, ny), f32),
        vmem((rows, ny), f32),
        vmem((3, rows, ny), f32),
        vmem(bc_flags.shape, jnp.int32),
        vmem((rows, ny), jnp.int32),
        vmem(coarse_inverse.shape, f32),
        vmem((9, 3, rows, ny), f32),
        vmem((3, cz_n, ny), f32),
        vmem((3, cz_n, ny), f32),
        vmem((3, cx_n, ny), f32),
        vmem((3, cx_n, ny), f32),
        vmem((2, 3, cx_n, ny), f32),
        vmem((2, 3, 2 * cz_n, ny), f32),
        vmem((2, 3, 2 * cz_n, ny), f32),
        vmem((2, 2, 3, cx_n, ny), f32),
        vmem((2, 2, 3, cx_n, ny), f32),
        vmem((2, 2, 2, 3, cx_n, ny), f32),
        vmem((2, 4, 3, 1, ny), f32),
        vmem((2, 4, 3, 1, ny), f32),
        vmem((cx_n, ny), f32),
        vmem((cz_n, ny), f32),
        vmem((cx_n, ny), f32),
        vmem((5, 1, rows, ny), f32),
        vmem((2, 1, cz_n, ny), f32),
        vmem((2, 1, cz_n, ny), f32),
        vmem((2, 1, cx_n, ny), f32),
        vmem((2, 1, cx_n, ny), f32),
        vmem((2, 2, 1, cx_n, ny), f32),
        *wide_set(f32),
        *wide_set(jnp.int32),
        vmem((1, cz_n, ny), f32),
        vmem((1, cz_n, ny), f32),
        vmem((1, cx_n, ny), f32),
        vmem((1, cx_n, ny), f32),
        vmem((2, 1, cx_n, ny), f32),
        vmem(coarse_inverse.shape, f32),
        vmem(coarse_inverse.shape, f32),
        vmem((7, rows, ny), f32),
        vmem((7, cz_n, ny), f32),
        vmem((7, cz_n, ny), f32),
        vmem((7, cx_n, ny), f32),
        vmem((7, cx_n, ny), f32),
        vmem((2, 7, cx_n, ny), f32),
        vmem((2, 1, 128), f32),
        vmem((2, n_gx - 1, 1, 128), f32),
        vmem((2, 1, 128), f32),
        vmem((2, n_gz - 1, 1, 128), f32),
        vmem((1, lanes), f32),
        vmem((n_gz - 1, 1, lanes), f32),
        vmem((n_gz, 1, lanes), f32),
        vmem((n_gz, 1, lanes), f32),
        dma((9, 4)),
        dma((9, 4)),
        dma((2,)),
        dma((2,)),
        dma((2, n_gx - 1)),
        dma((2,)),
        dma((2, n_gz - 1)),
        dma((2,)),
        dma((3 * n_gz - 1,)),
        dma((3,)),
        dma((7,)),
        dma((34,)),
        dma((34,)),
    ]
    spec = pl.BlockSpec(memory_space=pltpu.VMEM)
    velocity, pressure = pl.pallas_call(
        functools.partial(kernel, (n_gx, n_gz, cx_n, cz_n, ny, lanes)),
        out_shape=(
            jax.ShapeDtypeStruct((3, rows, ny), f32),
            jax.ShapeDtypeStruct((rows, ny), f32),
        ),
        in_specs=[pl.BlockSpec(memory_space=pltpu.HBM)] * 7,
        out_specs=(spec, spec),
        scratch_shapes=scratch,
        compiler_params=pltpu.CompilerParams(
            collective_id=0, has_side_effects=True, vmem_limit_bytes=48 * 1024 * 1024
        ),
        name="corrector",
    )(
        *[
            pltpu.with_memory_space_constraint(a, pltpu.HBM)
            for a in (
                velocity_old.reshape(3, rows, ny),
                source.reshape(3, rows, ny),
                diag_coef.reshape(rows, ny),
                face_coef.reshape(3, rows, ny),
                bc_flags,
                coarse_map.reshape(rows, ny),
                coarse_inverse,
            )
        ]
    )
    return velocity.reshape(3, cx_n, cz_n, ny), pressure.reshape(cx_n, cz_n, ny)


def solution(mesh):
    placed = (
        P(None, "gx", "gz", None),
        P(None, "gx", "gz", None),
        P("gx", "gz", None),
        P(None, "gx", "gz", None),
        P(None, "gx", "gz"),
        P("gx", "gz", None),
        P("gx", None),
    )
    return jax.shard_map(
        functools.partial(body, mesh.shape["gx"], mesh.shape["gz"]),
        mesh=mesh,
        in_specs=placed,
        out_specs=(P(None, "gx", "gz", None), P("gx", "gz", None)),
        check_vma=False,
    )
```
